256 devices in a mesh: ctx: 32 (over z, y), head: 8 (over x, core).
Axes of the slice: x: 4, y: 4, z: 8, core: 2. Of those that a mesh axis runs over, the one named last changes fastest.
Arguments:
- queries: bfloat16 [32, 512, 3072], P('ctx', None, 'head'), may hold values from -5 to 5
- key_rows: bfloat16 [32, 512, 3072], P('ctx', None, 'head'), may hold values from -5 to 5
- value_rows: bfloat16 [32, 512, 3072], P('ctx', None, 'head'), may hold values from -6 to 6
- out_grad: bfloat16 [32, 512, 3072], P('ctx', None, 'head'), may hold values from -6 to 6
- head_kind: int32 [24], replicated, may hold values from 0 to 1, as said below
- frame_band: int32 [24], replicated, may hold values from 1 to 31, as said below
Outputs:
- attended: bfloat16 [32, 512, 3072], P('ctx', None, 'head')
- query_grad: bfloat16 [32, 512, 3072], P('ctx', None, 'head')
- key_grad: bfloat16 [32, 512, 3072], P('ctx', None, 'head')
- value_grad: bfloat16 [32, 512, 3072], P('ctx', None, 'head')
The draws below stay inside these ranges and needn't reach their ends.
Inputs may be any that keep to these rules, and one draw needn't show every extreme that they name: `head_kind`: exactly 8 entries are 1. `frame_band`: entries of spatial heads are not used; some temporal head has the value 32 - 1.
All inputs are finite; a program needn't handle non-finite values.
Results may differ from the reference program's by a relative error of at most 0.024.
Values may be sent and summed in bfloat16 or wider, within the bound.
A program may use at most 64 MiB of HBM per device.

```python
import jax
import jax.numpy as jnp
from jax import lax

DH = 128
HEADS = 24
NSPATIAL = 8
POS = 512
FRAMES = 32


def draw_queries(key, part):
    shape = (FRAMES, POS, HEADS * DH)
    values = jax.random.truncated_normal(jax.random.fold_in(key, 1), -5.0, 5.0, shape, jnp.float32)
    return values.astype(jnp.bfloat16)


def draw_key_rows(key, part):
    shape = (FRAMES, POS, HEADS * DH)
    values = jax.random.truncated_normal(jax.random.fold_in(key, 2), -5.0, 5.0, shape, jnp.float32)
    return values.astype(jnp.bfloat16)


def head_order(key):
    return jax.random.permutation(jax.random.fold_in(key, 11), jnp.arange(HEADS, dtype=jnp.int32))


def draw_head_kind(key, part):
    return (head_order(key) < NSPATIAL).astype(jnp.int32)


def draw_frame_band(key, part):
    order = head_order(key)
    band_draw = jax.random.randint(jax.random.fold_in(key, 12), (HEADS,), 1, FRAMES, dtype=jnp.int32)
    return jnp.where(order == HEADS - 1, FRAMES - 1, band_draw).astype(jnp.int32)


def level_of(own_key, shape, split, low, high):
    factor_of, own = 1.0, jax.random.fold_in(own_key, 6)
    for dim, shards_of in split:
        steps = jnp.exp(jax.random.uniform(jax.random.fold_in(own, dim), (shards_of,), jnp.float32, low / len(split), high / len(split)))
        factor_of = factor_of * jnp.repeat(steps, shape[dim] // shards_of).reshape([-1 if axis == dim else 1 for axis in range(len(shape))])
    return factor_of


def centred(key, extent, scale, limit, split=(), held_as=jnp.bfloat16):
    entries = jax.random.normal(key, extent, jnp.float32) * scale
    if len(split) > 0:
        entries = level_of(key, extent, split, -0.22, 0.18) * entries
    return jnp.clip(entries, min=-limit, max=limit).astype(held_as)


def setup_inputs(seed: int = 0) -> dict:
    splits = jax.random.split(jax.random.key(seed), 7)
    return {
        "queries": draw_queries(jax.random.fold_in(splits[6], 71), 0),
        "key_rows": draw_key_rows(jax.random.fold_in(splits[6], 71), 0),
        "value_rows": centred(splits[2], (FRAMES, POS, HEADS * DH), 1.0, 6.0, ((0, 32), (2, 8))),
        "out_grad": centred(splits[3], (FRAMES, POS, HEADS * DH), 1.0, 6.0, ((0, 32), (2, 8))),
        "head_kind": draw_head_kind(jax.random.fold_in(splits[6], 71), 0),
        "frame_band": draw_frame_band(jax.random.fold_in(splits[6], 71), 0),
    }


def log_sum(scores):
    top_value = jnp.max(scores, axis=-1, keepdims=True)
    return top_value + jnp.log(jnp.sum(jnp.exp(scores - top_value), axis=-1, keepdims=True))


def spatial_frames(q_head, k_head, v_head, g_head, band_value):
    scaling = DH ** -0.5

    def one_frame(frame):
        earlier = jnp.maximum(frame - 1, 0)
        key_pair = jnp.concatenate([k_head[earlier], k_head[frame]], axis=0)
        value_pair = jnp.concatenate([v_head[earlier], v_head[frame]], axis=0)
        q_frame = q_head[frame]
        g_frame = g_head[frame]
        has_prior = jnp.broadcast_to(frame > 0, (POS,))
        valid = jnp.concatenate([has_prior, jnp.ones((POS,), dtype=bool)])[None, :]
        score = jnp.dot(q_frame, key_pair.T, preferred_element_type=jnp.float32) * scaling
        score = jnp.where(valid, score, -jnp.inf)
        weight = jnp.exp(score - log_sum(score))
        prob = weight.astype(jnp.bfloat16)
        attended = jnp.dot(prob, value_pair, preferred_element_type=jnp.float32).astype(jnp.bfloat16)
        delta = jnp.sum(g_frame.astype(jnp.float32) * attended.astype(jnp.float32), axis=-1, keepdims=True)
        dprob = jnp.dot(g_frame, value_pair.T, preferred_element_type=jnp.float32)
        dscore = (weight * (dprob - delta) * scaling).astype(jnp.bfloat16)
        q_grad = jnp.dot(dscore, key_pair, preferred_element_type=jnp.float32).astype(jnp.bfloat16)
        k_grad = jnp.dot(dscore.T, q_frame, preferred_element_type=jnp.float32)
        v_grad = jnp.dot(prob.T, g_frame, preferred_element_type=jnp.float32)
        return attended, q_grad, k_grad[POS:], k_grad[:POS], v_grad[POS:], v_grad[:POS]

    attended, q_grad, k_own, k_prior, v_own, v_prior = lax.map(one_frame, jnp.arange(FRAMES, dtype=jnp.int32))
    tail_rows = jnp.zeros((1, POS, DH), jnp.float32)
    k_grad = (k_own + jnp.concatenate([k_prior[1:], tail_rows], axis=0)).astype(jnp.bfloat16)
    v_grad = (v_own + jnp.concatenate([v_prior[1:], tail_rows], axis=0)).astype(jnp.bfloat16)
    return attended, q_grad, k_grad, v_grad


def temporal_frames(q_head, k_head, v_head, g_head, band_value):
    scaling = DH ** -0.5
    q_float = q_head.astype(jnp.float32)
    k_float = k_head.astype(jnp.float32)
    v_float = v_head.astype(jnp.float32)
    g_float = g_head.astype(jnp.float32)
    score = jnp.einsum("fpd,gpd->pfg", q_float, k_float) * scaling
    frame_ids = jnp.arange(FRAMES, dtype=jnp.int32)
    allowed = jnp.abs(frame_ids[:, None] - frame_ids[None, :]) <= band_value
    score = jnp.where(allowed[None], score, -jnp.inf)
    weight = jnp.exp(score - log_sum(score))
    prob = weight.astype(jnp.bfloat16)
    attended = jnp.einsum("pfg,gpd->fpd", prob.astype(jnp.float32), v_float).astype(jnp.bfloat16)
    delta = jnp.sum(g_float * attended.astype(jnp.float32), axis=-1)
    dprob = jnp.einsum("fpd,gpd->pfg", g_float, v_float)
    dscore = (weight * (dprob - delta.T[:, :, None]) * scaling).astype(jnp.bfloat16)
    dscore_float = dscore.astype(jnp.float32)
    q_grad = jnp.einsum("pfg,gpd->fpd", dscore_float, k_float).astype(jnp.bfloat16)
    k_grad = jnp.einsum("pfg,fpd->gpd", dscore_float, q_float).astype(jnp.bfloat16)
    v_grad = jnp.einsum("pfg,fpd->gpd", prob.astype(jnp.float32), g_float).astype(jnp.bfloat16)
    return attended, q_grad, k_grad, v_grad


def split_heads(rows):
    return jnp.transpose(rows.reshape(FRAMES, POS, HEADS, DH), (2, 0, 1, 3))


def join_heads(rows):
    return jnp.transpose(rows, (1, 2, 0, 3)).reshape(FRAMES, POS, HEADS * DH)


def reference(queries, key_rows, value_rows, out_grad, head_kind, frame_band):
    stacked = (split_heads(queries), split_heads(key_rows), split_heads(value_rows), split_heads(out_grad), head_kind, frame_band)

    def one_head(item):
        q_head, k_head, v_head, g_head, kind_value, band_value = item
        return lax.cond(kind_value == 1, spatial_frames, temporal_frames, q_head, k_head, v_head, g_head, band_value)

    results = lax.map(one_head, stacked)
    return join_heads(results[0]), join_heads(results[1]), join_heads(results[2]), join_heads(results[3])
```

```python
import functools
import math

import jax
import jax.numpy as jnp
from jax import lax
from jax.experimental import pallas as pl
from jax.experimental.pallas import tpu as pltpu
from jax.sharding import PartitionSpec as P

DH = 128
HEADS = 24
NSPATIAL = 8
NTEMPORAL = 16
MESH = pl.DeviceIdType.MESH
NEG = -1e30
SCALE = DH ** -0.5
LOG2E = math.log2(math.e)

F32 = jnp.float32
BF16 = jnp.bfloat16

CTX = 32
NY = 4
SH = 8
LH = 3
POS = 512
BLK = 64
SUB = 16
ROWS = CTX * SUB

Q, K, V, G = 0, 1, 2, 3
ATT, QG, KG, VG = 0, 1, 2, 3


def dot_t(a, b):
    return lax.dot_general(a, b, (((1,), (1,)), ((), ())), preferred_element_type=F32)


def dot_n(a, b):
    return lax.dot_general(a, b, (((1,), (0,)), ((), ())), preferred_element_type=F32)


def t_dot(a, b):
    return lax.dot_general(a, b, (((0,), (0,)), ((), ())), preferred_element_type=F32)


def await_bytes(ref, sem):
    pltpu.make_async_copy(ref, ref, sem).wait()


def kernel(
    kind_ref, band_ref, q_hbm, k_hbm, v_hbm, g_hbm,
    att_hbm, qg_hbm, kg_hbm, vg_hbm,
    lists, got0, got1, got2, got3, t_send, t_rows, s_send, s_rows, prior, prior_send, prior_back,
    reach, t_weight, t_prob, t_dscore, s_prob, s_dscore, t_out, s_out, back0, back1, back2, back3, home_send,
    f1_send, f1_recv, t_sent, t_recv, s_sent, s_recv, p_sent, p_recv, b_sent, b_recv,
    rt_sent, rs_sent, r_recv, h_sent, h_recv,
):
    c = lax.axis_index("ctx")
    h = lax.axis_index("head")
    z = lax.div(c, NY)
    inputs = (q_hbm, k_hbm, v_hbm, g_hbm)
    outputs = (att_hbm, qg_hbm, kg_hbm, vg_hbm)
    gathered = (got0, got1, got2, got3)
    results = (back0, back1, back2, back3)

    def ctx_peer(d):
        return lax.rem(c + d, CTX)

    def head_peer(d):
        return lax.rem(h + d, SH)

    def remote(src, dst, send, recv, ctx, head):
        pltpu.make_async_remote_copy(
            src_ref=src, dst_ref=dst, send_sem=send, recv_sem=recv,
            device_id=(ctx, head), device_id_type=MESH,
        ).start()

    barrier = pltpu.get_barrier_semaphore()

    @pl.loop(1, SH)
    def _(d):
        pl.semaphore_signal(barrier, inc=1, device_id=(c, head_peer(d)), device_id_type=MESH)

    @pl.loop(1, CTX)
    def _(d):
        pl.semaphore_signal(barrier, inc=1, device_id=(ctx_peer(d), h), device_id_type=MESH)

    for a in range(4):
        for i in range(LH):
            pltpu.make_async_copy(
                inputs[a].at[pl.ds(h * BLK, BLK), pl.ds(i * DH, DH)],
                gathered[a].at[LH * h + i], f1_recv.at[a],
            ).start()

    kinds = [kind_ref[i] for i in range(HEADS)]
    so_far, count = [], jnp.int32(0)
    limits = [jnp.int32(0), jnp.int32(0)]
    for i in range(HEADS):
        spatial = kinds[i] == 1
        slot = jnp.where(spatial, NTEMPORAL + i - count, count)
        lists[32 + i] = jnp.minimum(slot, HEADS - 1)
        for e in range(2):
            limits[e] = jnp.where(slot == 2 * z + e, band_ref[i] * SUB, limits[e])
        count = count + jnp.where(spatial, 0, 1)
        so_far.append(count)
    for t in range(NTEMPORAL):
        before = sum((jnp.where(so_far[i] <= t, 1, 0) for i in range(HEADS)), jnp.int32(0))
        lists[t] = jnp.minimum(before, HEADS - 1)
    for s in range(NSPATIAL):
        before = sum((jnp.where(i + 1 - so_far[i] <= s, 1, 0) for i in range(HEADS)), jnp.int32(0))
        lists[NTEMPORAL + s] = jnp.minimum(before, HEADS - 1)

    @pl.loop(0, ROWS // 64)
    def _(b):
        row = lax.broadcasted_iota(jnp.int32, (64, ROWS), 0) + b * 64
        col = lax.broadcasted_iota(jnp.int32, (64, ROWS), 1)
        apart = row - col
        reach[pl.ds(b * 64, 64), :] = jnp.where(
            (apart & (SUB - 1)) == 0, jnp.abs(apart), ROWS * 2
        ).astype(F32)

    pl.semaphore_wait(barrier, SH - 1 + CTX - 1)

    for a in range(4):
        @pl.loop(1, SH)
        def _(d):
            to = head_peer(d)
            for i in range(LH):
                remote(
                    inputs[a].at[pl.ds(to * BLK, BLK), pl.ds(i * DH, DH)],
                    gathered[a].at[LH * h + i], f1_send.at[a], f1_recv.at[a], c, to,
                )

    def block_of(a, slot):
        return gathered[a][lists[slot]]

    def select_and_send(a):
        await_bytes(gathered[a], f1_recv.at[a])
        for pair in range(NTEMPORAL // 2):
            for e in range(2):
                block = block_of(a, 2 * pair + e)
                for y in range(NY):
                    t_send[a, pair * NY + y, e] = block[y * SUB:(y + 1) * SUB]
        pltpu.make_async_copy(t_send.at[a, c], t_rows.at[a, c], t_recv.at[a]).start()

        @pl.loop(1, CTX)
        def _(d):
            to = ctx_peer(d)
            remote(t_send.at[a, to], t_rows.at[a, c], t_sent, t_recv.at[a], to, h)

        for s in range(NSPATIAL):
            s_send[a, s] = block_of(a, NTEMPORAL + s)
        pltpu.make_async_copy(s_send.at[a, h], s_rows.at[a, h], s_recv.at[a]).start()

        @pl.loop(1, SH)
        def _(d):
            to = head_peer(d)
            remote(s_send.at[a, to], s_rows.at[a, h], s_sent, s_recv.at[a], c, to)

    for a in (Q, K, V, G):
        select_and_send(a)

    await_bytes(s_rows.at[K], s_recv.at[K])
    await_bytes(s_rows.at[V], s_recv.at[V])
    remote(s_rows.at[K], prior.at[0], p_sent, p_recv, ctx_peer(1), h)
    remote(s_rows.at[V], prior.at[1], p_sent, p_recv, ctx_peer(1), h)

    def t_block(a, e, first, frames):
        return t_rows[a, pl.ds(first, frames), e].reshape(frames * SUB, DH)

    def t_all(a, e):
        return t_block(a, e, 0, CTX)

    await_bytes(t_rows.at[Q], t_recv.at[Q])
    await_bytes(t_rows.at[K], t_recv.at[K])
    for e in range(2):
        keys = t_all(K, e)
        for part in range(2):
            score = dot_t(t_block(Q, e, part * 16, 16), keys) * (SCALE * LOG2E)
            rows = pl.ds(part * 256, 256)
            score = score + jnp.minimum(limits[e].astype(F32) - reach[rows, :], 0.0) * -NEG
            top = jnp.max(score, axis=-1, keepdims=True)
            weight = jnp.exp2(score - top)
            weight = weight * (1.0 / jnp.sum(weight, axis=-1, keepdims=True))
            t_weight[e, rows, :] = weight
            t_prob[e, rows, :] = weight.astype(BF16)

    await_bytes(s_rows.at[Q], s_recv.at[Q])
    await_bytes(s_rows.at[G], s_recv.at[G])
    await_bytes(prior, p_recv)
    k_own = s_rows[K].reshape(POS, DH)
    v_own = s_rows[V].reshape(POS, DH)
    k_prior = prior[0].reshape(POS, DH)
    v_prior = prior[1].reshape(POS, DH)
    part_rows = 128
    part_blocks = part_rows // BLK

    @pl.loop(0, POS // part_rows)
    def _(part):
        rows = pl.ds(part * part_rows, part_rows)
        blocks = pl.ds(part * part_blocks, part_blocks)
        q = s_rows[Q, blocks].reshape(part_rows, DH)
        g = s_rows[G, blocks].reshape(part_rows, DH)
        old = dot_t(q, k_prior) * (SCALE * LOG2E)
        old = jnp.where(c > 0, old, NEG)
        own = dot_t(q, k_own) * (SCALE * LOG2E)
        top = jnp.maximum(
            jnp.max(old, axis=-1, keepdims=True), jnp.max(own, axis=-1, keepdims=True)
        )
        old = jnp.exp2(old - top)
        own = jnp.exp2(own - top)
        inverse = 1.0 / (
            jnp.sum(old, axis=-1, keepdims=True) + jnp.sum(own, axis=-1, keepdims=True)
        )
        old = old * inverse
        own = own * inverse
        old_prob = old.astype(BF16)
        own_prob = own.astype(BF16)
        s_prob[0, rows, :] = old_prob
        s_prob[1, rows, :] = own_prob
        attended = (dot_n(old_prob, v_prior) + dot_n(own_prob, v_own)).astype(BF16)
        s_out[ATT, blocks] = attended.reshape(part_blocks, NY, SUB, DH)
        delta = jnp.sum(g.astype(F32) * attended.astype(F32), axis=-1, keepdims=True)
        old_ds = (old * (dot_t(g, v_prior) - delta) * SCALE).astype(BF16)
        own_ds = (own * (dot_t(g, v_own) - delta) * SCALE).astype(BF16)
        s_dscore[0, rows, :] = old_ds
        s_dscore[1, rows, :] = own_ds
        qg = (dot_n(old_ds, k_prior) + dot_n(own_ds, k_own)).astype(BF16)
        s_out[QG, blocks] = qg.reshape(part_blocks, NY, SUB, DH)

    q_all = s_rows[Q].reshape(POS, DH)
    g_all = s_rows[G].reshape(POS, DH)
    prior_send[0] = t_dot(s_dscore[0], q_all).astype(BF16)
    prior_send[1] = t_dot(s_prob[0], g_all).astype(BF16)
    remote(prior_send, prior_back, b_sent, b_recv, ctx_peer(CTX - 1), h)

    def send_spatial(o):
        pltpu.make_async_copy(s_out.at[o, h], results[o].at[NTEMPORAL + h], r_recv.at[o]).start()

        @pl.loop(1, SH)
        def _(d):
            to = head_peer(d)
            remote(
                s_out.at[o, to], results[o].at[NTEMPORAL + h], rs_sent, r_recv.at[o], c, to
            )

    send_spatial(ATT)
    send_spatial(QG)

    def send_temporal(o):
        mine = results[o].at[pl.ds(2 * z, 2), lax.rem(c, NY)]
        pltpu.make_async_copy(t_out.at[o, c], mine, r_recv.at[o]).start()

        @pl.loop(1, CTX)
        def _(d):
            to = ctx_peer(d)
            remote(t_out.at[o, to], mine, rt_sent, r_recv.at[o], to, h)

    def put(o, e, value):
        t_out[o, :, e] = value.astype(BF16).reshape(CTX, SUB, DH)

    await_bytes(t_rows.at[V], t_recv.at[V])
    for e in range(2):
        put(ATT, e, dot_n(t_prob[e], t_all(V, e)))
    send_temporal(ATT)

    k_total = t_dot(s_dscore[1], q_all)
    v_total = t_dot(s_prob[1], g_all)
    await_bytes(prior_back, b_recv)
    k_total = (k_total + prior_back[0].astype(F32)).astype(BF16)
    v_total = (v_total + prior_back[1].astype(F32)).astype(BF16)
    s_out[KG] = k_total.reshape(SH, NY, SUB, DH)
    s_out[VG] = v_total.reshape(SH, NY, SUB, DH)
    send_spatial(VG)
    send_spatial(KG)

    await_bytes(t_rows.at[G], t_recv.at[G])
    for e in range(2):
        put(VG, e, t_dot(t_prob[e], t_all(G, e)))
    send_temporal(VG)
    for e in range(2):
        values = t_all(V, e)
        keys = t_all(K, e)
        for part in range(2):
            rows = pl.ds(part * 256, 256)
            g = t_block(G, e, part * 16, 16)
            attended = t_out[ATT, pl.ds(part * 16, 16), e].reshape(256, DH)
            delta = jnp.sum(g.astype(F32) * attended.astype(F32), axis=-1, keepdims=True)
            dscore = t_weight[e, rows, :] * (dot_t(g, values) - delta) * SCALE
            t_dscore[e, rows, :] = dscore.astype(BF16)
        put(QG, e, dot_n(t_dscore[e], keys))
    send_temporal(QG)
    for e in range(2):
        put(KG, e, t_dot(t_dscore[e], t_all(Q, e)))
    send_temporal(KG)

    for o in (ATT, VG, QG, KG):
        await_bytes(results[o], r_recv.at[o])
        for head in range(HEADS):
            block = results[o][lists[32 + head]].reshape(BLK, DH)
            shard, column = divmod(head, LH)
            home_send[o, shard, :, column * DH:(column + 1) * DH] = block
        mine = pl.ds(h * BLK, BLK)
        pltpu.make_async_copy(home_send.at[o, h], outputs[o].at[mine, :], h_recv.at[o]).start()

        @pl.loop(1, SH)
        def _(d):
            to = head_peer(d)
            remote(home_send.at[o, to], outputs[o].at[mine, :], h_sent, h_recv.at[o], c, to)

    for o in range(4):
        await_bytes(outputs[o], h_recv.at[o])
    for a in range(4):
        await_bytes(gathered[a].at[pl.ds(0, HEADS - LH)], f1_send.at[a])
    await_bytes(t_rows.at[:, pl.ds(0, CTX - 1)], t_sent)
    await_bytes(s_rows.at[:, pl.ds(0, SH - 1)], s_sent)
    await_bytes(prior, p_sent)
    await_bytes(prior_send, b_sent)
    await_bytes(t_out.at[:, pl.ds(0, CTX - 1)], rt_sent)
    await_bytes(s_out.at[:, pl.ds(0, SH - 1)], rs_sent)
    await_bytes(home_send.at[:, pl.ds(0, SH - 1)], h_sent)


def body(queries, key_rows, value_rows, out_grad, head_kind, frame_band):
    width = LH * DH
    local = [x.reshape(POS, width) for x in (queries, key_rows, value_rows, out_grad)]
    vmem = pltpu.VMEM
    dma = pltpu.SemaphoreType.DMA
    outs = pl.pallas_call(
        kernel,
        out_shape=[jax.ShapeDtypeStruct((POS, width), BF16)] * 4,
        in_specs=[pl.BlockSpec(memory_space=pltpu.SMEM)] * 2
        + [pl.BlockSpec(memory_space=pl.ANY)] * 4,
        out_specs=[pl.BlockSpec(memory_space=pl.ANY)] * 4,
        scratch_shapes=[
            pltpu.SMEM((64,), jnp.int32),
            *[vmem((HEADS, BLK, DH), BF16)] * 4,
            vmem((4, CTX, 2, SUB, DH), BF16),
            vmem((4, CTX, 2, SUB, DH), BF16),
            vmem((4, SH, BLK, DH), BF16),
            vmem((4, SH, BLK, DH), BF16),
            vmem((2, SH, BLK, DH), BF16),
            vmem((2, POS, DH), BF16),
            vmem((2, POS, DH), BF16),
            vmem((ROWS, ROWS), F32),
            vmem((2, ROWS, ROWS), F32),
            vmem((2, ROWS, ROWS), BF16),
            vmem((2, ROWS, ROWS), BF16),
            vmem((2, POS, POS), BF16),
            vmem((2, POS, POS), BF16),
            vmem((4, CTX, 2, SUB, DH), BF16),
            vmem((4, SH, NY, SUB, DH), BF16),
            *[vmem((HEADS, NY, SUB, DH), BF16)] * 4,
            vmem((4, SH, BLK, width), BF16),
            dma((4,)), dma((4,)), dma, dma((4,)), dma, dma((4,)), dma, dma, dma, dma,
            dma, dma, dma((4,)), dma, dma((4,)),
        ],
        compiler_params=pltpu.CompilerParams(
            collective_id=0, has_side_effects=True, vmem_limit_bytes=56 << 20
        ),
        name="video_attention",
    )(head_kind, frame_band, *local)
    return tuple(x[None] for x in outs)


def solution(mesh):
    rows = P("ctx", None, "head")
    return jax.shard_map(
        body,
        mesh=mesh,
        in_specs=(rows, rows, rows, rows, P(), P()),
        out_specs=(rows, rows, rows, rows),
        check_vma=False,
    )
```

```python
import functools
import math

import jax
import jax.numpy as jnp
from jax import lax
from jax.experimental import pallas as pl
from jax.experimental.pallas import tpu as pltpu
from jax.sharding import PartitionSpec as P

DH = 128
HEADS = 24
NSPATIAL = 8
NTEMPORAL = 16
MESH = pl.DeviceIdType.MESH
NEG = -1e30
SCALE = DH ** -0.5
LOG2E = math.log2(math.e)

F32 = jnp.float32
BF16 = jnp.bfloat16

CTX = 32
NY = 4
SH = 8
LH = 3
POS = 512
BLK = 64
SUB = 16
ROWS = CTX * SUB

Q, K, V, G = 0, 1, 2, 3
ATT, QG, KG, VG = 0, 1, 2, 3


def dot_t(a, b):
    return lax.dot_general(a, b, (((1,), (1,)), ((), ())), preferred_element_type=F32)


def dot_n(a, b):
    return lax.dot_general(a, b, (((1,), (0,)), ((), ())), preferred_element_type=F32)


def t_dot(a, b):
    return lax.dot_general(a, b, (((0,), (0,)), ((), ())), preferred_element_type=F32)


def await_bytes(ref, sem):
    pltpu.make_async_copy(ref, ref, sem).wait()


def kernel(
    kind_ref, band_ref, q_hbm, k_hbm, v_hbm, g_hbm,
    att_hbm, qg_hbm, kg_hbm, vg_hbm,
    lists, got0, got1, got2, got3, t_send, t_rows, s_send, s_rows, prior, prior_send, prior_back,
    reach, t_weight, t_prob, t_dscore, s_prob, s_dscore, t_out, s_out, back0, back1, back2, back3, home_send,
    f1_send, f1_recv, t_sent, t_recv, s_sent, s_recv, p_sent, p_recv, b_sent, b_recv,
    rt_sent, rs_sent, r_recv, h_sent, h_recv, row_sem,
):
    c = lax.axis_index("ctx")
    h = lax.axis_index("head")
    z = lax.div(c, NY)
    inputs = (q_hbm, k_hbm, v_hbm, g_hbm)
    outputs = (att_hbm, qg_hbm, kg_hbm, vg_hbm)
    gathered = (got0, got1, got2, got3)
    results = (back0, back1, back2, back3)

    def ctx_peer(d):
        return lax.rem(c + d, CTX)

    def head_peer(d):
        return lax.rem(h + d, SH)

    def remote(src, dst, send, recv, ctx, head):
        pltpu.make_async_remote_copy(
            src_ref=src, dst_ref=dst, send_sem=send, recv_sem=recv,
            device_id=(ctx, head), device_id_type=MESH,
        ).start()

    barrier = pltpu.get_barrier_semaphore()

    @pl.loop(1, SH)
    def _(d):
        pl.semaphore_signal(barrier, inc=1, device_id=(c, head_peer(d)), device_id_type=MESH)

    y = lax.rem(c, NY)

    def y_peer(d):
        return z * NY + lax.rem(y + d, NY)

    @pl.loop(1, CTX // NY)
    def _(d):
        pl.semaphore_signal(
            barrier, inc=1, device_id=(ctx_peer(d * NY), h), device_id_type=MESH
        )

    @pl.loop(1, NY)
    def _(d):
        pl.semaphore_signal(barrier, inc=1, device_id=(y_peer(d), h), device_id_type=MESH)

    for a in range(4):
        for i in range(LH):
            pltpu.make_async_copy(
                inputs[a].at[pl.ds(h * BLK, BLK), pl.ds(i * DH, DH)],
                gathered[a].at[LH * h + i], f1_recv.at[a],
            ).start()

    kinds = [kind_ref[i] for i in range(HEADS)]
    so_far, count = [], jnp.int32(0)
    limits = [jnp.int32(0), jnp.int32(0)]
    for i in range(HEADS):
        spatial = kinds[i] == 1
        slot = jnp.where(spatial, NTEMPORAL + i - count, count)
        lists[32 + i] = jnp.minimum(slot, HEADS - 1)
        for e in range(2):
            limits[e] = jnp.where(slot == 2 * z + e, band_ref[i] * SUB, limits[e])
        count = count + jnp.where(spatial, 0, 1)
        so_far.append(count)
    for t in range(NTEMPORAL):
        before = sum((jnp.where(so_far[i] <= t, 1, 0) for i in range(HEADS)), jnp.int32(0))
        lists[t] = jnp.minimum(before, HEADS - 1)
    for s in range(NSPATIAL):
        before = sum((jnp.where(i + 1 - so_far[i] <= s, 1, 0) for i in range(HEADS)), jnp.int32(0))
        lists[NTEMPORAL + s] = jnp.minimum(before, HEADS - 1)

    @pl.loop(0, ROWS // 64)
    def _(b):
        row = lax.broadcasted_iota(jnp.int32, (64, ROWS), 0) + b * 64
        col = lax.broadcasted_iota(jnp.int32, (64, ROWS), 1)
        apart = row - col
        reach[pl.ds(b * 64, 64), :] = jnp.where(
            (apart & (SUB - 1)) == 0, jnp.abs(apart), ROWS * 2
        ).astype(F32)

    pl.semaphore_wait(barrier, SH - 1 + CTX // NY - 1 + NY - 1)

    for a in range(4):
        @pl.loop(1, SH)
        def _(d):
            to = head_peer(d)
            for i in range(LH):
                remote(
                    inputs[a].at[pl.ds(to * BLK, BLK), pl.ds(i * DH, DH)],
                    gathered[a].at[LH * h + i], f1_send.at[a], f1_recv.at[a], c, to,
                )

    @pl.loop(1, NY)
    def _(d):
        pl.semaphore_signal(row_sem, inc=1, device_id=(y_peer(d), h), device_id_type=MESH)

    pl.semaphore_wait(row_sem, NY - 1)

    def block_of(a, slot):
        return gathered[a][lists[slot]]

    def select_and_send(a):
        await_bytes(gathered[a], f1_recv.at[a])
        for pair in range(NTEMPORAL // 2):
            for e in range(2):
                block = block_of(a, 2 * pair + e)
                for y in range(NY):
                    t_send[a, pair * NY + y, e] = block[y * SUB:(y + 1) * SUB]
        pltpu.make_async_copy(t_send.at[a, c], t_rows.at[a, c], t_recv.at[a]).start()

        @pl.loop(1, CTX)
        def _(d):
            to = ctx_peer(d)
            remote(t_send.at[a, to], t_rows.at[a, c], t_sent, t_recv.at[a], to, h)

        for s in range(NSPATIAL):
            s_send[a, s] = block_of(a, NTEMPORAL + s)
        pltpu.make_async_copy(s_send.at[a, h], s_rows.at[a, h], s_recv.at[a]).start()

        @pl.loop(1, SH)
        def _(d):
            to = head_peer(d)
            remote(s_send.at[a, to], s_rows.at[a, h], s_sent, s_recv.at[a], c, to)

    for a in (K, V, Q):
        select_and_send(a)
    await_bytes(s_rows.at[K], s_recv.at[K])
    await_bytes(s_rows.at[V], s_recv.at[V])
    remote(s_rows.at[K], prior.at[0], p_sent, p_recv, ctx_peer(1), h)
    remote(s_rows.at[V], prior.at[1], p_sent, p_recv, ctx_peer(1), h)
    select_and_send(G)

    def t_block(a, e, first, frames):
        return t_rows[a, pl.ds(first, frames), e].reshape(frames * SUB, DH)

    def t_all(a, e):
        return t_block(a, e, 0, CTX)

    def send_temporal(o):
        mine = results[o].at[pl.ds(2 * z, 2), lax.rem(c, NY)]
        pltpu.make_async_copy(t_out.at[o, c], mine, r_recv.at[o]).start()

        @pl.loop(1, CTX)
        def _(d):
            to = ctx_peer(d)
            remote(t_out.at[o, to], mine, rt_sent, r_recv.at[o], to, h)

    def put(o, e, value):
        t_out[o, :, e] = value.astype(BF16).reshape(CTX, SUB, DH)

    await_bytes(t_rows.at[K], t_recv.at[K])
    await_bytes(t_rows.at[Q], t_recv.at[Q])
    for e in range(2):
        keys = t_all(K, e)
        for part in range(2):
            score = dot_t(t_block(Q, e, part * 16, 16), keys) * (SCALE * LOG2E)
            rows = pl.ds(part * 256, 256)
            score = score + jnp.minimum(limits[e].astype(F32) - reach[rows, :], 0.0) * -NEG
            top = jnp.max(score, axis=-1, keepdims=True)
            weight = jnp.exp2(score - top)
            weight = weight * (1.0 / jnp.sum(weight, axis=-1, keepdims=True))
            t_weight[e, rows, :] = weight
            t_prob[e, rows, :] = weight.astype(BF16)
    await_bytes(t_rows.at[V], t_recv.at[V])
    for e in range(2):
        put(ATT, e, dot_n(t_prob[e], t_all(V, e)))
    send_temporal(ATT)

    await_bytes(s_rows.at[Q], s_recv.at[Q])
    await_bytes(s_rows.at[G], s_recv.at[G])
    await_bytes(prior, p_recv)
    k_own = s_rows[K].reshape(POS, DH)
    v_own = s_rows[V].reshape(POS, DH)
    k_prior = prior[0].reshape(POS, DH)
    v_prior = prior[1].reshape(POS, DH)
    part_rows = 256
    part_blocks = part_rows // BLK

    @pl.loop(0, POS // part_rows)
    def _(part):
        rows = pl.ds(part * part_rows, part_rows)
        blocks = pl.ds(part * part_blocks, part_blocks)
        q = s_rows[Q, blocks].reshape(part_rows, DH)
        g = s_rows[G, blocks].reshape(part_rows, DH)
        old = dot_t(q, k_prior) * (SCALE * LOG2E)
        old = jnp.where(c > 0, old, NEG)
        own = dot_t(q, k_own) * (SCALE * LOG2E)
        top = jnp.maximum(
            jnp.max(old, axis=-1, keepdims=True), jnp.max(own, axis=-1, keepdims=True)
        )
        old = jnp.exp2(old - top)
        own = jnp.exp2(own - top)
        inverse = 1.0 / (
            jnp.sum(old, axis=-1, keepdims=True) + jnp.sum(own, axis=-1, keepdims=True)
        )
        old = old * inverse
        own = own * inverse
        old_prob = old.astype(BF16)
        own_prob = own.astype(BF16)
        s_prob[0, rows, :] = old_prob
        s_prob[1, rows, :] = own_prob
        attended = (dot_n(old_prob, v_prior) + dot_n(own_prob, v_own)).astype(BF16)
        s_out[ATT, blocks] = attended.reshape(part_blocks, NY, SUB, DH)
        delta = jnp.sum(g.astype(F32) * attended.astype(F32), axis=-1, keepdims=True)
        old_ds = (old * (dot_t(g, v_prior) - delta) * SCALE).astype(BF16)
        own_ds = (own * (dot_t(g, v_own) - delta) * SCALE).astype(BF16)
        s_dscore[0, rows, :] = old_ds
        s_dscore[1, rows, :] = own_ds
        qg = (dot_n(old_ds, k_prior) + dot_n(own_ds, k_own)).astype(BF16)
        s_out[QG, blocks] = qg.reshape(part_blocks, NY, SUB, DH)

    def send_spatial(o):
        pltpu.make_async_copy(s_out.at[o, h], results[o].at[NTEMPORAL + h], r_recv.at[o]).start()

        @pl.loop(1, SH)
        def _(d):
            to = head_peer(d)
            remote(
                s_out.at[o, to], results[o].at[NTEMPORAL + h], rs_sent, r_recv.at[o], c, to
            )

    q_all = s_rows[Q].reshape(POS, DH)
    g_all = s_rows[G].reshape(POS, DH)
    prior_send[0] = t_dot(s_dscore[0], q_all).astype(BF16)
    prior_send[1] = t_dot(s_prob[0], g_all).astype(BF16)
    remote(prior_send, prior_back, b_sent, b_recv, ctx_peer(CTX - 1), h)
    send_spatial(ATT)
    send_spatial(QG)
    await_bytes(t_rows.at[G], t_recv.at[G])
    for e in range(2):
        put(VG, e, t_dot(t_prob[e], t_all(G, e)))
    send_temporal(VG)
    for e in range(2):
        values = t_all(V, e)
        keys = t_all(K, e)
        for part in range(2):
            rows = pl.ds(part * 256, 256)
            g = t_block(G, e, part * 16, 16)
            attended = t_out[ATT, pl.ds(part * 16, 16), e].reshape(256, DH)
            delta = jnp.sum(g.astype(F32) * attended.astype(F32), axis=-1, keepdims=True)
            dscore = t_weight[e, rows, :] * (dot_t(g, values) - delta) * SCALE
            t_dscore[e, rows, :] = dscore.astype(BF16)
        put(QG, e, dot_n(t_dscore[e], keys))
    send_temporal(QG)
    for e in range(2):
        put(KG, e, t_dot(t_dscore[e], t_all(Q, e)))
    send_temporal(KG)

    k_total = t_dot(s_dscore[1], q_all)
    v_total = t_dot(s_prob[1], g_all)
    await_bytes(prior_back, b_recv)
    k_total = (k_total + prior_back[0].astype(F32)).astype(BF16)
    v_total = (v_total + prior_back[1].astype(F32)).astype(BF16)
    s_out[KG] = k_total.reshape(SH, NY, SUB, DH)
    s_out[VG] = v_total.reshape(SH, NY, SUB, DH)
    send_spatial(VG)
    send_spatial(KG)

    for o in (ATT, VG, QG, KG):
        await_bytes(results[o], r_recv.at[o])
        for head in range(HEADS):
            block = results[o][lists[32 + head]].reshape(BLK, DH)
            shard, column = divmod(head, LH)
            home_send[o, shard, :, column * DH:(column + 1) * DH] = block
        mine = pl.ds(h * BLK, BLK)
        pltpu.make_async_copy(home_send.at[o, h], outputs[o].at[mine, :], h_recv.at[o]).start()

        @pl.loop(1, SH)
        def _(d):
            to = head_peer(d)
            remote(home_send.at[o, to], outputs[o].at[mine, :], h_sent, h_recv.at[o], c, to)

    for o in range(4):
        await_bytes(outputs[o], h_recv.at[o])
    for a in range(4):
        await_bytes(gathered[a].at[pl.ds(0, HEADS - LH)], f1_send.at[a])
    await_bytes(t_rows.at[:, pl.ds(0, CTX - 1)], t_sent)
    await_bytes(s_rows.at[:, pl.ds(0, SH - 1)], s_sent)
    await_bytes(prior, p_sent)
    await_bytes(prior_send, b_sent)
    await_bytes(t_out.at[:, pl.ds(0, CTX - 1)], rt_sent)
    await_bytes(s_out.at[:, pl.ds(0, SH - 1)], rs_sent)
    await_bytes(home_send.at[:, pl.ds(0, SH - 1)], h_sent)


def copy_kernel(*refs):
    sources, targets, held, in_sem, out_sem = refs[:4], refs[4:8], refs[8], refs[9], refs[10]
    reads = [pltpu.make_async_copy(x, held.at[o], in_sem.at[o]) for o, x in enumerate(sources)]
    writes = [pltpu.make_async_copy(held.at[o], x, out_sem.at[o]) for o, x in enumerate(targets)]
    for read in reads:
        read.start()
    for read, write in zip(reads, writes):
        read.wait()
        write.start()
    for write in writes:
        write.wait()


def body(queries, key_rows, value_rows, out_grad, head_kind, frame_band):
    width = LH * DH
    local = [x.reshape(POS, width) for x in (queries, key_rows, value_rows, out_grad)]
    vmem = pltpu.VMEM
    dma = pltpu.SemaphoreType.DMA
    outs = pl.pallas_call(
        kernel,
        out_shape=[jax.ShapeDtypeStruct((POS, width), BF16)] * 4,
        in_specs=[pl.BlockSpec(memory_space=pltpu.SMEM)] * 2
        + [pl.BlockSpec(memory_space=pl.ANY)] * 4,
        out_specs=[pl.BlockSpec(memory_space=pl.ANY)] * 4,
        scratch_shapes=[
            pltpu.SMEM((64,), jnp.int32),
            *[vmem((HEADS, BLK, DH), BF16)] * 4,
            vmem((4, CTX, 2, SUB, DH), BF16),
            vmem((4, CTX, 2, SUB, DH), BF16),
            vmem((4, SH, BLK, DH), BF16),
            vmem((4, SH, BLK, DH), BF16),
            vmem((2, SH, BLK, DH), BF16),
            vmem((2, POS, DH), BF16),
            vmem((2, POS, DH), BF16),
            vmem((ROWS, ROWS), F32),
            vmem((2, ROWS, ROWS), F32),
            vmem((2, ROWS, ROWS), BF16),
            vmem((2, ROWS, ROWS), BF16),
            vmem((2, POS, POS), BF16),
            vmem((2, POS, POS), BF16),
            vmem((4, CTX, 2, SUB, DH), BF16),
            vmem((4, SH, NY, SUB, DH), BF16),
            *[vmem((HEADS, NY, SUB, DH), BF16)] * 4,
            vmem((4, SH, BLK, width), BF16),
            dma((4,)), dma((4,)), dma, dma((4,)), dma, dma((4,)), dma, dma, dma, dma,
            dma, dma, dma((4,)), dma, dma((4,)), pltpu.SemaphoreType.REGULAR,
        ],
        compiler_params=pltpu.CompilerParams(
            collective_id=0, has_side_effects=True, vmem_limit_bytes=56 << 20
        ),
        name="video_attention",
    )(head_kind, frame_band, *local)
    outs = pl.pallas_call(
        copy_kernel,
        out_shape=[jax.ShapeDtypeStruct((POS, width), BF16)] * 4,
        in_specs=[pl.BlockSpec(memory_space=pl.ANY)] * 4,
        out_specs=[pl.BlockSpec(memory_space=pl.ANY)] * 4,
        scratch_shapes=[vmem((4, POS, width), BF16), dma((4,)), dma((4,))],
        compiler_params=pltpu.CompilerParams(vmem_limit_bytes=56 << 20),
        name="copy_results",
    )(*outs)
    return tuple(x[None] for x in outs)


def solution(mesh):
    rows = P("ctx", None, "head")
    return jax.shard_map(
        body,
        mesh=mesh,
        in_specs=(rows, rows, rows, rows, P(), P()),
        out_specs=(rows, rows, rows, rows),
        check_vma=False,
    )
```

```python
import functools
import math

import jax
import jax.numpy as jnp
from jax import lax
from jax.experimental import pallas as pl
from jax.experimental.pallas import tpu as pltpu
from jax.sharding import PartitionSpec as P

DH = 128
HEADS = 24
NSPATIAL = 8
NTEMPORAL = 16
MESH = pl.DeviceIdType.MESH
NEG = -1e30
SCALE = DH ** -0.5
LOG2E = math.log2(math.e)

F32 = jnp.float32
BF16 = jnp.bfloat16

CTX = 32
NY = 4
SH = 8
LH = 3
POS = 512
BLK = 64
SUB = 16
ROWS = CTX * SUB

Q, K, V, G = 0, 1, 2, 3
ATT, QG, KG, VG = 0, 1, 2, 3
CHUNKS = ((K, 0, 32), (K, 32, 32), (V, 0, 64), (Q, 0, 64), (G, 0, 64))


def dot_t(a, b):
    return lax.dot_general(a, b, (((1,), (1,)), ((), ())), preferred_element_type=F32)


def dot_n(a, b):
    return lax.dot_general(a, b, (((1,), (0,)), ((), ())), preferred_element_type=F32)


def t_dot(a, b):
    return lax.dot_general(a, b, (((0,), (0,)), ((), ())), preferred_element_type=F32)


def await_bytes(ref, sem):
    pltpu.make_async_copy(ref, ref, sem).wait()


def kernel(
    kind_ref, band_ref, q_hbm, k_hbm, v_hbm, g_hbm,
    att_hbm, qg_hbm, kg_hbm, vg_hbm,
    lists, got0, got1, got2, got3, got4, t_send, t_rows, s_send, s_rows, prior, prior_send, prior_back, relay_up, relay_down,
    reach, t_weight, t_prob, t_dscore, s_prob, s_dscore, t_out, s_out, back0, back1, back2, back3, home_send,
    f1_send, f1_recv, t_sent, t_recv, s_sent, s_recv, p_sent, p_recv, b_sent, b_recv,
    rt_sent, rs_sent, r_recv, h_sent, h_recv, up_sent, up_recv, down_sent, down_recv, row_sem,
):
    c = lax.axis_index("ctx")
    h = lax.axis_index("head")
    z = lax.div(c, NY)
    inputs = (q_hbm, k_hbm, v_hbm, g_hbm)
    outputs = (att_hbm, qg_hbm, kg_hbm, vg_hbm)
    gathered = (got0, got1, got2, got3, got4)
    results = (back0, back1, back2, back3)

    def ctx_peer(d):
        return lax.rem(c + d, CTX)

    def head_peer(d):
        return lax.rem(h + d, SH)

    def remote(src, dst, send, recv, ctx, head):
        pltpu.make_async_remote_copy(
            src_ref=src, dst_ref=dst, send_sem=send, recv_sem=recv,
            device_id=(ctx, head), device_id_type=MESH,
        ).start()

    barrier = pltpu.get_barrier_semaphore()

    @pl.loop(1, SH)
    def _(d):
        pl.semaphore_signal(barrier, inc=1, device_id=(c, head_peer(d)), device_id_type=MESH)

    y = lax.rem(c, NY)

    def y_peer(d):
        return z * NY + lax.rem(y + d, NY)

    @pl.loop(1, CTX // NY)
    def _(d):
        pl.semaphore_signal(
            barrier, inc=1, device_id=(ctx_peer(d * NY), h), device_id_type=MESH
        )

    @pl.loop(1, NY)
    def _(d):
        pl.semaphore_signal(barrier, inc=1, device_id=(y_peer(d), h), device_id_type=MESH)

    def piece(n, shard, i):
        a, first, count = CHUNKS[n]
        return inputs[a].at[pl.ds(shard * BLK + first, count), pl.ds(i * DH, DH)]

    for n in range(len(CHUNKS)):
        for i in range(LH):
            pltpu.make_async_copy(
                piece(n, h, i), gathered[n].at[LH * h + i], f1_recv.at[n]
            ).start()

    kinds = [kind_ref[i] for i in range(HEADS)]
    so_far, count = [], jnp.int32(0)
    limits = [jnp.int32(0), jnp.int32(0)]
    for i in range(HEADS):
        spatial = kinds[i] == 1
        slot = jnp.where(spatial, NTEMPORAL + i - count, count)
        lists[32 + i] = jnp.minimum(slot, HEADS - 1)
        for e in range(2):
            limits[e] = jnp.where(slot == 2 * z + e, band_ref[i] * SUB, limits[e])
        count = count + jnp.where(spatial, 0, 1)
        so_far.append(count)
    for t in range(NTEMPORAL):
        before = sum((jnp.where(so_far[i] <= t, 1, 0) for i in range(HEADS)), jnp.int32(0))
        lists[t] = jnp.minimum(before, HEADS - 1)
    for s in range(NSPATIAL):
        before = sum((jnp.where(i + 1 - so_far[i] <= s, 1, 0) for i in range(HEADS)), jnp.int32(0))
        lists[NTEMPORAL + s] = jnp.minimum(before, HEADS - 1)

    @pl.loop(0, ROWS // 64)
    def _(b):
        row = lax.broadcasted_iota(jnp.int32, (64, ROWS), 0) + b * 64
        col = lax.broadcasted_iota(jnp.int32, (64, ROWS), 1)
        apart = row - col
        reach[pl.ds(b * 64, 64), :] = jnp.where(
            (apart & (SUB - 1)) == 0, jnp.abs(apart), ROWS * 2
        ).astype(F32)

    pl.semaphore_wait(barrier, SH - 1 + CTX // NY - 1 + NY - 1)

    for n in range(len(CHUNKS)):
        @pl.loop(1, SH)
        def _(d):
            to = head_peer(d)
            for i in range(LH):
                remote(
                    piece(n, to, i), gathered[n].at[LH * h + i],
                    f1_send.at[n], f1_recv.at[n], c, to,
                )

    @pl.loop(1, NY)
    def _(d):
        pl.semaphore_signal(row_sem, inc=1, device_id=(y_peer(d), h), device_id_type=MESH)

    pl.semaphore_wait(row_sem, NY - 1)

    def select_and_send(n):
        a, first, count = CHUNKS[n]
        subs = range(first // SUB, (first + count) // SUB)
        await_bytes(gathered[n], f1_recv.at[n])
        for pair in range(NTEMPORAL // 2):
            for e in range(2):
                block = gathered[n][lists[2 * pair + e]]
                for at, sub in enumerate(subs):
                    t_send[a, pair * NY + sub, e] = block[at * SUB:(at + 1) * SUB]

        @pl.loop(0, CTX // NY)
        def _(d):
            for sub in subs:
                to = lax.rem(z + d, CTX // NY) * NY + sub

                @pl.when(to == c)
                def _():
                    pltpu.make_async_copy(t_send.at[a, c], t_rows.at[a, c], t_recv.at[a]).start()

                @pl.when(to != c)
                def _():
                    remote(t_send.at[a, to], t_rows.at[a, c], t_sent, t_recv.at[a], to, h)

        for s in range(NSPATIAL):
            s_send[a, s, pl.ds(first, count)] = gathered[n][lists[NTEMPORAL + s]]
        if first + count == BLK:
            pltpu.make_async_copy(s_send.at[a, h], s_rows.at[a, h], s_recv.at[a]).start()

            @pl.loop(1, SH)
            def _(d):
                to = head_peer(d)
                remote(s_send.at[a, to], s_rows.at[a, h], s_sent, s_recv.at[a], c, to)

    for n in range(len(CHUNKS) - 1):
        select_and_send(n)
    await_bytes(s_rows.at[K], s_recv.at[K])
    await_bytes(s_rows.at[V], s_recv.at[V])
    pairs = [pl.ds(2 * r, 2) for r in range(NY)]

    @pl.when(y < NY - 1)
    def _():
        remote(s_rows.at[pl.ds(K, 2)], prior, p_sent, p_recv, ctx_peer(1), h)

    @pl.when(y == NY - 1)
    def _():
        for r in range(NY - 1):
            remote(s_rows.at[pl.ds(K, 2), pairs[r]], relay_up, p_sent, up_recv, z * NY + r, h)
        last = pairs[NY - 1]
        remote(s_rows.at[pl.ds(K, 2), last], prior.at[:, last], p_sent, p_recv, ctx_peer(1), h)

    select_and_send(len(CHUNKS) - 1)

    @pl.when(y < NY - 1)
    def _():
        await_bytes(relay_up, up_recv)
        above = lax.rem(z + 1, CTX // NY) * NY
        remote(relay_up, prior.at[:, pl.ds(2 * y, 2)], up_sent, p_recv, above, h)

    def t_block(a, e, first, frames):
        return t_rows[a, pl.ds(first, frames), e].reshape(frames * SUB, DH)

    def t_all(a, e):
        return t_block(a, e, 0, CTX)

    def send_temporal(o):
        mine = results[o].at[pl.ds(2 * z, 2), lax.rem(c, NY)]
        pltpu.make_async_copy(t_out.at[o, c], mine, r_recv.at[o]).start()

        @pl.loop(1, CTX)
        def _(d):
            to = ctx_peer(d)
            remote(t_out.at[o, to], mine, rt_sent, r_recv.at[o], to, h)

    def put(o, e, value):
        t_out[o, :, e] = value.astype(BF16).reshape(CTX, SUB, DH)

    await_bytes(t_rows.at[K], t_recv.at[K])
    await_bytes(t_rows.at[Q], t_recv.at[Q])
    for e in range(2):
        keys = t_all(K, e)
        for part in range(2):
            score = dot_t(t_block(Q, e, part * 16, 16), keys) * (SCALE * LOG2E)
            rows = pl.ds(part * 256, 256)
            score = score + jnp.minimum(limits[e].astype(F32) - reach[rows, :], 0.0) * -NEG
            top = jnp.max(score, axis=-1, keepdims=True)
            weight = jnp.exp2(score - top)
            weight = weight * (1.0 / jnp.sum(weight, axis=-1, keepdims=True))
            t_weight[e, rows, :] = weight
            t_prob[e, rows, :] = weight.astype(BF16)
    await_bytes(t_rows.at[V], t_recv.at[V])
    for e in range(2):
        put(ATT, e, dot_n(t_prob[e], t_all(V, e)))
    send_temporal(ATT)

    await_bytes(s_rows.at[Q], s_recv.at[Q])
    await_bytes(s_rows.at[G], s_recv.at[G])
    await_bytes(prior, p_recv)
    k_own = s_rows[K].reshape(POS, DH)
    v_own = s_rows[V].reshape(POS, DH)
    k_prior = prior[0].reshape(POS, DH)
    v_prior = prior[1].reshape(POS, DH)
    part_rows = 256
    part_blocks = part_rows // BLK

    @pl.loop(0, POS // part_rows)
    def _(part):
        rows = pl.ds(part * part_rows, part_rows)
        blocks = pl.ds(part * part_blocks, part_blocks)
        q = s_rows[Q, blocks].reshape(part_rows, DH)
        g = s_rows[G, blocks].reshape(part_rows, DH)
        old = dot_t(q, k_prior) * (SCALE * LOG2E)
        old = jnp.where(c > 0, old, NEG)
        own = dot_t(q, k_own) * (SCALE * LOG2E)
        top = jnp.maximum(
            jnp.max(old, axis=-1, keepdims=True), jnp.max(own, axis=-1, keepdims=True)
        )
        old = jnp.exp2(old - top)
        own = jnp.exp2(own - top)
        inverse = 1.0 / (
            jnp.sum(old, axis=-1, keepdims=True) + jnp.sum(own, axis=-1, keepdims=True)
        )
        old = old * inverse
        own = own * inverse
        old_prob = old.astype(BF16)
        own_prob = own.astype(BF16)
        s_prob[0, rows, :] = old_prob
        s_prob[1, rows, :] = own_prob
        attended = (dot_n(old_prob, v_prior) + dot_n(own_prob, v_own)).astype(BF16)
        s_out[ATT, blocks] = attended.reshape(part_blocks, NY, SUB, DH)
        delta = jnp.sum(g.astype(F32) * attended.astype(F32), axis=-1, keepdims=True)
        old_ds = (old * (dot_t(g, v_prior) - delta) * SCALE).astype(BF16)
        own_ds = (own * (dot_t(g, v_own) - delta) * SCALE).astype(BF16)
        s_dscore[0, rows, :] = old_ds
        s_dscore[1, rows, :] = own_ds
        qg = (dot_n(old_ds, k_prior) + dot_n(own_ds, k_own)).astype(BF16)
        s_out[QG, blocks] = qg.reshape(part_blocks, NY, SUB, DH)

    def send_spatial(o):
        pltpu.make_async_copy(s_out.at[o, h], results[o].at[NTEMPORAL + h], r_recv.at[o]).start()

        @pl.loop(1, SH)
        def _(d):
            to = head_peer(d)
            remote(
                s_out.at[o, to], results[o].at[NTEMPORAL + h], rs_sent, r_recv.at[o], c, to
            )

    q_all = s_rows[Q].reshape(POS, DH)
    g_all = s_rows[G].reshape(POS, DH)
    prior_send[0] = t_dot(s_dscore[0], q_all).astype(BF16).reshape(SH, BLK, DH)
    prior_send[1] = t_dot(s_prob[0], g_all).astype(BF16).reshape(SH, BLK, DH)

    @pl.when(y > 0)
    def _():
        remote(prior_send, prior_back, b_sent, b_recv, ctx_peer(CTX - 1), h)

    @pl.when(y == 0)
    def _():
        own = pairs[0]
        remote(prior_send.at[:, own], prior_back.at[:, own], b_sent, b_recv, ctx_peer(CTX - 1), h)
        for r in range(1, NY):
            remote(prior_send.at[:, pairs[r]], relay_down, b_sent, down_recv, z * NY + r, h)

    send_spatial(ATT)
    send_spatial(QG)
    await_bytes(t_rows.at[G], t_recv.at[G])
    for e in range(2):
        values = t_all(V, e)
        keys = t_all(K, e)
        for part in range(2):
            rows = pl.ds(part * 256, 256)
            g = t_block(G, e, part * 16, 16)
            attended = t_out[ATT, pl.ds(part * 16, 16), e].reshape(256, DH)
            delta = jnp.sum(g.astype(F32) * attended.astype(F32), axis=-1, keepdims=True)
            dscore = t_weight[e, rows, :] * (dot_t(g, values) - delta) * SCALE
            t_dscore[e, rows, :] = dscore.astype(BF16)
        put(QG, e, dot_n(t_dscore[e], keys))
    send_temporal(QG)
    @pl.when(y > 0)
    def _():
        await_bytes(relay_down, down_recv)
        below = lax.rem(z + CTX // NY - 1, CTX // NY) * NY + NY - 1
        remote(relay_down, prior_back.at[:, pl.ds(2 * y, 2)], down_sent, b_recv, below, h)

    for e in range(2):
        put(VG, e, t_dot(t_prob[e], t_all(G, e)))
    send_temporal(VG)

    def send_home(o):
        await_bytes(results[o], r_recv.at[o])
        for head in range(HEADS):
            block = results[o][lists[32 + head]].reshape(BLK, DH)
            shard, column = divmod(head, LH)
            home_send[o, shard, :, column * DH:(column + 1) * DH] = block
        mine = pl.ds(h * BLK, BLK)
        pltpu.make_async_copy(home_send.at[o, h], outputs[o].at[mine, :], h_recv.at[o]).start()

        @pl.loop(1, SH)
        def _(d):
            to = head_peer(d)
            remote(home_send.at[o, to], outputs[o].at[mine, :], h_sent, h_recv.at[o], c, to)

    for e in range(2):
        put(KG, e, t_dot(t_dscore[e], t_all(Q, e)))
    send_home(ATT)
    send_temporal(KG)

    send_home(QG)
    k_total = t_dot(s_dscore[1], q_all)
    v_total = t_dot(s_prob[1], g_all)
    await_bytes(prior_back, b_recv)
    k_total = (k_total + prior_back[0].reshape(POS, DH).astype(F32)).astype(BF16)
    v_total = (v_total + prior_back[1].reshape(POS, DH).astype(F32)).astype(BF16)
    s_out[KG] = k_total.reshape(SH, NY, SUB, DH)
    s_out[VG] = v_total.reshape(SH, NY, SUB, DH)
    send_spatial(VG)
    send_spatial(KG)

    send_home(VG)
    send_home(KG)

    for o in range(4):
        await_bytes(outputs[o], h_recv.at[o])
    for n in range(len(CHUNKS)):
        await_bytes(gathered[n].at[pl.ds(0, HEADS - LH)], f1_send.at[n])
    await_bytes(t_rows.at[:, pl.ds(0, CTX - 1)], t_sent)
    await_bytes(s_rows.at[:, pl.ds(0, SH - 1)], s_sent)
    await_bytes(prior, p_sent)
    await_bytes(prior_send, b_sent)

    @pl.when(y < NY - 1)
    def _():
        await_bytes(relay_up, up_sent)

    @pl.when(y > 0)
    def _():
        await_bytes(relay_down, down_sent)

    await_bytes(t_out.at[:, pl.ds(0, CTX - 1)], rt_sent)
    await_bytes(s_out.at[:, pl.ds(0, SH - 1)], rs_sent)
    await_bytes(home_send.at[:, pl.ds(0, SH - 1)], h_sent)


def copy_kernel(*refs):
    sources, targets, held, in_sem, out_sem = refs[:4], refs[4:8], refs[8], refs[9], refs[10]
    reads = [pltpu.make_async_copy(x, held.at[o], in_sem.at[o]) for o, x in enumerate(sources)]
    writes = [pltpu.make_async_copy(held.at[o], x, out_sem.at[o]) for o, x in enumerate(targets)]
    for read in reads:
        read.start()
    for read, write in zip(reads, writes):
        read.wait()
        write.start()
    for write in writes:
        write.wait()


def body(queries, key_rows, value_rows, out_grad, head_kind, frame_band):
    width = LH * DH
    local = [x.reshape(POS, width) for x in (queries, key_rows, value_rows, out_grad)]
    vmem = pltpu.VMEM
    dma = pltpu.SemaphoreType.DMA
    outs = pl.pallas_call(
        kernel,
        out_shape=[jax.ShapeDtypeStruct((POS, width), BF16)] * 4,
        in_specs=[pl.BlockSpec(memory_space=pltpu.SMEM)] * 2
        + [pl.BlockSpec(memory_space=pl.ANY)] * 4,
        out_specs=[pl.BlockSpec(memory_space=pl.ANY)] * 4,
        scratch_shapes=[
            pltpu.SMEM((64,), jnp.int32),
            *[vmem((HEADS, count, DH), BF16) for _, _, count in CHUNKS],
            vmem((4, CTX, 2, SUB, DH), BF16),
            vmem((4, CTX, 2, SUB, DH), BF16),
            vmem((4, SH, BLK, DH), BF16),
            vmem((4, SH, BLK, DH), BF16),
            vmem((2, SH, BLK, DH), BF16),
            vmem((2, SH, BLK, DH), BF16),
            vmem((2, SH, BLK, DH), BF16),
            vmem((2, 2, BLK, DH), BF16),
            vmem((2, 2, BLK, DH), BF16),
            vmem((ROWS, ROWS), F32),
            vmem((2, ROWS, ROWS), F32),
            vmem((2, ROWS, ROWS), BF16),
            vmem((2, ROWS, ROWS), BF16),
            vmem((2, POS, POS), BF16),
            vmem((2, POS, POS), BF16),
            vmem((4, CTX, 2, SUB, DH), BF16),
            vmem((4, SH, NY, SUB, DH), BF16),
            *[vmem((HEADS, NY, SUB, DH), BF16)] * 4,
            vmem((4, SH, BLK, width), BF16),
            dma((len(CHUNKS),)), dma((len(CHUNKS),)),
            dma, dma((4,)), dma, dma((4,)), dma, dma, dma, dma,
            dma, dma, dma((4,)), dma, dma((4,)), dma, dma, dma, dma, pltpu.SemaphoreType.REGULAR,
        ],
        compiler_params=pltpu.CompilerParams(
            collective_id=0, has_side_effects=True, vmem_limit_bytes=56 << 20
        ),
        name="video_attention",
    )(head_kind, frame_band, *local)
    outs = pl.pallas_call(
        copy_kernel,
        out_shape=[jax.ShapeDtypeStruct((POS, width), BF16)] * 4,
        in_specs=[pl.BlockSpec(memory_space=pl.ANY)] * 4,
        out_specs=[pl.BlockSpec(memory_space=pl.ANY)] * 4,
        scratch_shapes=[vmem((4, POS, width), BF16), dma((4,)), dma((4,))],
        compiler_params=pltpu.CompilerParams(vmem_limit_bytes=56 << 20),
        name="copy_results",
    )(*outs)
    return tuple(x[None] for x in outs)


def solution(mesh):
    rows = P("ctx", None, "head")
    return jax.shard_map(
        body,
        mesh=mesh,
        in_specs=(rows, rows, rows, rows, P(), P()),
        out_specs=(rows, rows, rows, rows),
        check_vma=False,
    )
```

```python
import functools
import math

import jax
import jax.numpy as jnp
from jax import lax
from jax.experimental import pallas as pl
from jax.experimental.pallas import tpu as pltpu
from jax.sharding import PartitionSpec as P

DH = 128
HEADS = 24
NSPATIAL = 8
NTEMPORAL = 16
MESH = pl.DeviceIdType.MESH
NEG = -1e30
SCALE = DH ** -0.5
LOG2E = math.log2(math.e)

F32 = jnp.float32
BF16 = jnp.bfloat16

CTX = 32
NY = 4
SH = 8
LH = 3
POS = 512
BLK = 64
SUB = 16
ROWS = CTX * SUB

Q, K, V, G = 0, 1, 2, 3
ATT, QG, KG, VG = 0, 1, 2, 3
Z_ORDER = (4, 3, 5, 2, 6, 1, 7, 0)
CHUNKS = ((K, 0, 32), (K, 32, 32), (V, 0, 64), (Q, 0, 64), (G, 0, 64))


def dot_t(a, b):
    return lax.dot_general(a, b, (((1,), (1,)), ((), ())), preferred_element_type=F32)


def dot_n(a, b):
    return lax.dot_general(a, b, (((1,), (0,)), ((), ())), preferred_element_type=F32)


def t_dot(a, b):
    return lax.dot_general(a, b, (((0,), (0,)), ((), ())), preferred_element_type=F32)


def await_bytes(ref, sem):
    pltpu.make_async_copy(ref, ref, sem).wait()


def kernel(
    kind_ref, band_ref, q_hbm, k_hbm, v_hbm, g_hbm,
    att_hbm, qg_hbm, kg_hbm, vg_hbm,
    lists, got0, got1, got2, got3, got4, t_send, t_rows, s_send, s_rows, prior, prior_send, k_back, v_back, relay_up, relay_down,
    reach, t_weight, t_prob, t_dscore, s_prob, s_dscore, t_out, s_out, back0, back1, back2, back3, home_send,
    f1_send, f1_recv, t_sent, t_recv, s_sent, s_recv, p_sent, p_recv, b_sent, b_recv,
    rt_sent, rs_sent, r_recv, h_sent, h_recv, up_sent, up_recv, down_sent, down_recv, met,
):
    c = lax.axis_index("ctx")
    h = lax.axis_index("head")
    z = lax.div(c, NY)
    inputs = (q_hbm, k_hbm, v_hbm, g_hbm)
    outputs = (att_hbm, qg_hbm, kg_hbm, vg_hbm)
    gathered = (got0, got1, got2, got3, got4)
    results = (back0, back1, back2, back3)

    def ctx_peer(d):
        return lax.rem(c + d, CTX)

    def head_peer(d):
        return lax.rem(h + d, SH)

    def remote(src, dst, send, recv, ctx, head):
        pltpu.make_async_remote_copy(
            src_ref=src, dst_ref=dst, send_sem=send, recv_sem=recv,
            device_id=(ctx, head), device_id_type=MESH,
        ).start()

    barrier = pltpu.get_barrier_semaphore()

    @pl.loop(1, SH)
    def _(d):
        pl.semaphore_signal(barrier, inc=1, device_id=(c, head_peer(d)), device_id_type=MESH)

    y = lax.rem(c, NY)

    def y_peer(d):
        return z * NY + lax.rem(y + d, NY)

    def z_peer(d):
        return lax.rem(c + d * NY + CTX, CTX)

    for d in (1, -1):
        pl.semaphore_signal(barrier, inc=1, device_id=(z_peer(d), h), device_id_type=MESH)

    @pl.loop(1, NY)
    def _(d):
        pl.semaphore_signal(barrier, inc=1, device_id=(y_peer(d), h), device_id_type=MESH)

    pl.semaphore_wait(barrier, SH - 1 + 2 + NY - 1)

    def piece(n, shard, i):
        a, first, count = CHUNKS[n]
        return inputs[a].at[pl.ds(shard * BLK + first, count), pl.ds(i * DH, DH)]

    for n in range(len(CHUNKS)):
        @pl.loop(1, SH)
        def _(d):
            to = head_peer(d)
            for i in range(LH):
                remote(
                    piece(n, to, i), gathered[n].at[LH * h + i],
                    f1_send.at[n], f1_recv.at[n], c, to,
                )

    for n in range(len(CHUNKS)):
        for i in range(LH):
            pltpu.make_async_copy(
                piece(n, h, i), gathered[n].at[LH * h + i], f1_recv.at[n]
            ).start()

    kinds = [kind_ref[i] for i in range(HEADS)]
    so_far, count = [], jnp.int32(0)
    limits = [jnp.int32(0), jnp.int32(0)]
    for i in range(HEADS):
        spatial = kinds[i] == 1
        slot = jnp.where(spatial, NTEMPORAL + i - count, count)
        slot_in = jnp.minimum(slot, HEADS - 1)
        lists[32 + i] = slot_in
        lists[64 + i] = jnp.where(spatial, slot_in - NTEMPORAL, NSPATIAL)
        for e in range(2):
            limits[e] = jnp.where(slot == 2 * z + e, band_ref[i] * SUB, limits[e])
        count = count + jnp.where(spatial, 0, 1)
        so_far.append(count)
    for t in range(NTEMPORAL):
        before = sum((jnp.where(so_far[i] <= t, 1, 0) for i in range(HEADS)), jnp.int32(0))
        lists[t] = jnp.minimum(before, HEADS - 1)
    for s in range(NSPATIAL):
        before = sum((jnp.where(i + 1 - so_far[i] <= s, 1, 0) for i in range(HEADS)), jnp.int32(0))
        lists[NTEMPORAL + s] = jnp.minimum(before, HEADS - 1)

    @pl.loop(0, ROWS // 64)
    def _(b):
        row = lax.broadcasted_iota(jnp.int32, (64, ROWS), 0) + b * 64
        col = lax.broadcasted_iota(jnp.int32, (64, ROWS), 1)
        apart = row - col
        reach[pl.ds(b * 64, 64), :] = jnp.where(
            (apart & (SUB - 1)) == 0, jnp.abs(apart), ROWS * 2
        ).astype(F32)

    for far in (1, 2):
        for d in (far, -far):
            pl.semaphore_signal(
                met.at[far - 1], inc=1, device_id=(z_peer(d), h), device_id_type=MESH
            )
        pl.semaphore_wait(met.at[far - 1], 2)

    @pl.loop(1, NY)
    def _(d):
        pl.semaphore_signal(met.at[2], inc=1, device_id=(y_peer(d), h), device_id_type=MESH)

    pl.semaphore_wait(met.at[2], NY - 1)

    def select_and_send(n):
        a, first, count = CHUNKS[n]
        subs = range(first // SUB, (first + count) // SUB)
        await_bytes(gathered[n], f1_recv.at[n])
        for pair in range(NTEMPORAL // 2):
            for e in range(2):
                block = gathered[n][lists[2 * pair + e]]
                for at, sub in enumerate(subs):
                    t_send[a, pair * NY + sub, e] = block[at * SUB:(at + 1) * SUB]

        for dz in Z_ORDER:
            @pl.loop(0, len(subs))
            def _(k):
                to = lax.rem(z + dz, CTX // NY) * NY + subs[0] + k
                if dz == 0:
                    @pl.when(to == c)
                    def _():
                        pltpu.make_async_copy(
                            t_send.at[a, c], t_rows.at[a, c], t_recv.at[a]
                        ).start()

                @pl.when(to != c)
                def _():
                    remote(t_send.at[a, to], t_rows.at[a, c], t_sent, t_recv.at[a], to, h)

        for s in range(NSPATIAL):
            block = gathered[n][lists[NTEMPORAL + s]]
            s_send[a, s, pl.ds(subs[0], len(subs))] = block.reshape(len(subs), SUB, DH)
        if first + count < BLK:
            return
        pltpu.make_async_copy(s_send.at[a, h], s_rows.at[a, h], s_recv.at[a]).start()

        @pl.loop(1, SH)
        def _(d):
            to = head_peer(d)
            remote(s_send.at[a, to], s_rows.at[a, h], s_sent, s_recv.at[a], c, to)

    above = lax.rem(z + 1, CTX // NY) * NY
    below = lax.rem(z + CTX // NY - 1, CTX // NY) * NY + NY - 1

    def send_prior(a):
        i = a - K

        @pl.when(y < NY - 1)
        def _():
            @pl.loop(0, SH)
            def _(s):
                remote(s_send.at[a, s], prior.at[i, h], p_sent, p_recv, ctx_peer(1), s)

        @pl.when(y == NY - 1)
        def _():
            for r in range(NY - 1):
                remote(s_send.at[a, :, r], relay_up.at[i], p_sent, up_recv.at[i], z * NY + r, h)

            @pl.loop(0, SH)
            def _(s):
                remote(
                    s_send.at[a, s, NY - 1], prior.at[i, h, NY - 1], p_sent, p_recv, above, s
                )

    def pass_up(a):
        i = a - K

        @pl.when(y < NY - 1)
        def _():
            await_bytes(relay_up.at[i], up_recv.at[i])

            @pl.loop(0, SH)
            def _(s):
                remote(relay_up.at[i, s], prior.at[i, h, y], up_sent, p_recv, above, s)

    select_and_send(0)
    select_and_send(1)
    send_prior(K)
    select_and_send(2)
    send_prior(V)
    pass_up(K)
    select_and_send(3)
    pass_up(V)
    select_and_send(4)

    def t_block(a, e, first, frames):
        return t_rows[a, pl.ds(first, frames), e].reshape(frames * SUB, DH)

    def t_all(a, e):
        return t_block(a, e, 0, CTX)

    def send_temporal(o):
        mine = results[o].at[pl.ds(2 * z, 2), lax.rem(c, NY)]
        pltpu.make_async_copy(t_out.at[o, c], mine, r_recv.at[o]).start()

        for dz in Z_ORDER:
            @pl.loop(0 if dz else 1, NY)
            def _(k):
                to = lax.rem(z + dz, CTX // NY) * NY + lax.rem(y + k, NY)
                remote(t_out.at[o, to], mine, rt_sent, r_recv.at[o], to, h)

    def put(o, e, value):
        t_out[o, :, e] = value.astype(BF16).reshape(CTX, SUB, DH)

    await_bytes(t_rows.at[K], t_recv.at[K])
    await_bytes(t_rows.at[Q], t_recv.at[Q])
    for e in range(2):
        keys = t_all(K, e)
        for part in range(2):
            score = dot_t(t_block(Q, e, part * 16, 16), keys) * (SCALE * LOG2E)
            rows = pl.ds(part * 256, 256)
            score = score + jnp.minimum(limits[e].astype(F32) - reach[rows, :], 0.0) * -NEG
            top = jnp.max(score, axis=-1, keepdims=True)
            weight = jnp.exp2(score - top)
            weight = weight * (1.0 / jnp.sum(weight, axis=-1, keepdims=True))
            t_weight[e, rows, :] = weight
            t_prob[e, rows, :] = weight.astype(BF16)
    await_bytes(t_rows.at[V], t_recv.at[V])
    for e in range(2):
        put(ATT, e, dot_n(t_prob[e], t_all(V, e)))
    send_temporal(ATT)

    for a in range(4):
        await_bytes(s_rows.at[a], s_recv.at[a])
    await_bytes(prior, p_recv)
    k_own = s_rows[K].reshape(POS, DH)
    v_own = s_rows[V].reshape(POS, DH)
    k_prior = prior[0].reshape(POS, DH)
    v_prior = prior[1].reshape(POS, DH)
    part_rows = 256
    part_blocks = part_rows // BLK

    @pl.loop(0, POS // part_rows)
    def _(part):
        rows = pl.ds(part * part_rows, part_rows)
        blocks = pl.ds(part * part_blocks, part_blocks)
        q = s_rows[Q, blocks].reshape(part_rows, DH)
        g = s_rows[G, blocks].reshape(part_rows, DH)
        old = dot_t(q, k_prior) * (SCALE * LOG2E)
        old = jnp.where(c > 0, old, NEG)
        own = dot_t(q, k_own) * (SCALE * LOG2E)
        top = jnp.maximum(
            jnp.max(old, axis=-1, keepdims=True), jnp.max(own, axis=-1, keepdims=True)
        )
        old = jnp.exp2(old - top)
        own = jnp.exp2(own - top)
        inverse = 1.0 / (
            jnp.sum(old, axis=-1, keepdims=True) + jnp.sum(own, axis=-1, keepdims=True)
        )
        old = old * inverse
        own = own * inverse
        old_prob = old.astype(BF16)
        own_prob = own.astype(BF16)
        s_prob[0, rows, :] = old_prob
        s_prob[1, rows, :] = own_prob
        attended = (dot_n(old_prob, v_prior) + dot_n(own_prob, v_own)).astype(BF16)
        s_out[ATT, blocks] = attended.reshape(part_blocks, NY, SUB, DH)
        delta = jnp.sum(g.astype(F32) * attended.astype(F32), axis=-1, keepdims=True)
        old_ds = (old * (dot_t(g, v_prior) - delta) * SCALE).astype(BF16)
        own_ds = (own * (dot_t(g, v_own) - delta) * SCALE).astype(BF16)
        s_dscore[0, rows, :] = old_ds
        s_dscore[1, rows, :] = own_ds
        qg = (dot_n(old_ds, k_prior) + dot_n(own_ds, k_own)).astype(BF16)
        s_out[QG, blocks] = qg.reshape(part_blocks, NY, SUB, DH)

    def send_spatial(o):
        pltpu.make_async_copy(s_out.at[o, h], results[o].at[NTEMPORAL + h], r_recv.at[o]).start()

        @pl.loop(1, SH)
        def _(d):
            to = head_peer(d)
            remote(
                s_out.at[o, to], results[o].at[NTEMPORAL + h], rs_sent, r_recv.at[o], c, to
            )

    q_all = s_rows[Q].reshape(POS, DH)
    g_all = s_rows[G].reshape(POS, DH)
    prior_send[0] = t_dot(s_dscore[0], q_all).astype(BF16).reshape(SH, NY, SUB, DH)
    prior_send[1] = t_dot(s_prob[0], g_all).astype(BF16).reshape(SH, NY, SUB, DH)
    for i, back in enumerate((k_back, v_back)):
        @pl.when(y > 0)
        def _():
            @pl.loop(0, SH)
            def _(s):
                remote(prior_send.at[i, s], back.at[h], b_sent, b_recv.at[i], ctx_peer(CTX - 1), s)

        @pl.when(y == 0)
        def _():
            for r in range(1, NY):
                remote(
                    prior_send.at[i, :, r], relay_down.at[i], b_sent, down_recv, z * NY + r, h
                )

            @pl.loop(0, SH)
            def _(s):
                remote(prior_send.at[i, s, 0], back.at[h, 0], b_sent, b_recv.at[i], below, s)

    s_out[KG] = t_dot(s_dscore[1], q_all).astype(BF16).reshape(SH, NY, SUB, DH)
    s_out[VG] = t_dot(s_prob[1], g_all).astype(BF16).reshape(SH, NY, SUB, DH)
    for o in (ATT, QG, VG, KG):
        send_spatial(o)

    await_bytes(t_rows.at[G], t_recv.at[G])
    for e in range(2):
        values = t_all(V, e)
        keys = t_all(K, e)
        for part in range(2):
            rows = pl.ds(part * 256, 256)
            g = t_block(G, e, part * 16, 16)
            attended = t_out[ATT, pl.ds(part * 16, 16), e].reshape(256, DH)
            delta = jnp.sum(g.astype(F32) * attended.astype(F32), axis=-1, keepdims=True)
            dscore = t_weight[e, rows, :] * (dot_t(g, values) - delta) * SCALE
            t_dscore[e, rows, :] = dscore.astype(BF16)
        put(QG, e, dot_n(t_dscore[e], keys))
    send_temporal(QG)
    @pl.when(y > 0)
    def _():
        await_bytes(relay_down, down_recv)
        for i, back in enumerate((k_back, v_back)):
            @pl.loop(0, SH)
            def _(s):
                remote(relay_down.at[i, s], back.at[h, y], down_sent, b_recv.at[i], below, s)

    for e in range(2):
        put(VG, e, t_dot(t_prob[e], t_all(G, e)))
    send_temporal(VG)

    def send_home(o):
        await_bytes(results[o], r_recv.at[o])
        for head in range(HEADS):
            block = results[o][lists[32 + head]].reshape(BLK, DH)
            if o in (KG, VG):
                back = (k_back if o == KG else v_back)[lists[64 + head]].reshape(BLK, DH)
                block = (block.astype(F32) + back.astype(F32)).astype(BF16)
            shard, column = divmod(head, LH)
            home_send[o, shard, :, column * DH:(column + 1) * DH] = block
        mine = pl.ds(h * BLK, BLK)
        pltpu.make_async_copy(home_send.at[o, h], outputs[o].at[mine, :], h_recv.at[o]).start()

        @pl.loop(1, SH)
        def _(d):
            to = head_peer(d)
            remote(home_send.at[o, to], outputs[o].at[mine, :], h_sent, h_recv.at[o], c, to)

    for e in range(2):
        put(KG, e, t_dot(t_dscore[e], t_all(Q, e)))
    send_home(ATT)
    send_temporal(KG)

    send_home(QG)
    for back in (k_back, v_back):
        back[NSPATIAL] = jnp.zeros((NY, SUB, DH), BF16)
    for i, back in enumerate((k_back, v_back)):
        await_bytes(back.at[pl.ds(0, NSPATIAL)], b_recv.at[i])
    send_home(VG)
    send_home(KG)

    for o in range(4):
        await_bytes(outputs[o], h_recv.at[o])
    for n in range(len(CHUNKS)):
        await_bytes(gathered[n].at[pl.ds(0, HEADS - LH)], f1_send.at[n])
    await_bytes(t_rows.at[:, pl.ds(0, CTX - 1)], t_sent)
    await_bytes(s_rows.at[:, pl.ds(0, SH - 1)], s_sent)
    await_bytes(prior, p_sent)
    await_bytes(prior_send, b_sent)

    @pl.when(y < NY - 1)
    def _():
        await_bytes(relay_up, up_sent)

    @pl.when(y > 0)
    def _():
        await_bytes(relay_down, down_sent)

    await_bytes(t_out.at[:, pl.ds(0, CTX - 1)], rt_sent)
    await_bytes(s_out.at[:, pl.ds(0, SH - 1)], rs_sent)
    await_bytes(home_send.at[:, pl.ds(0, SH - 1)], h_sent)


def copy_kernel(*refs):
    sources, targets, sem = refs[:4], refs[4:8], refs[8]
    copies = [pltpu.make_async_copy(x, y, sem.at[o]) for o, (x, y) in enumerate(zip(sources, targets))]
    for copy in copies:
        copy.start()
    for copy in copies:
        copy.wait()


def body(queries, key_rows, value_rows, out_grad, head_kind, frame_band):
    width = LH * DH
    local = [x.reshape(POS, width) for x in (queries, key_rows, value_rows, out_grad)]
    vmem = pltpu.VMEM
    dma = pltpu.SemaphoreType.DMA
    outs = pl.pallas_call(
        kernel,
        out_shape=[jax.ShapeDtypeStruct((POS, width), BF16)] * 4,
        in_specs=[pl.BlockSpec(memory_space=pltpu.SMEM)] * 2
        + [pl.BlockSpec(memory_space=pl.ANY)] * 4,
        out_specs=[pl.BlockSpec(memory_space=pl.ANY)] * 4,
        scratch_shapes=[
            pltpu.SMEM((96,), jnp.int32),
            *[vmem((HEADS, count, DH), BF16) for _, _, count in CHUNKS],
            vmem((4, CTX, 2, SUB, DH), BF16),
            vmem((4, CTX, 2, SUB, DH), BF16),
            vmem((4, SH, NY, SUB, DH), BF16),
            vmem((4, SH, NY, SUB, DH), BF16),
            vmem((2, SH, NY, SUB, DH), BF16),
            vmem((2, SH, NY, SUB, DH), BF16),
            *[vmem((NSPATIAL + 1, NY, SUB, DH), BF16)] * 2,
            vmem((2, SH, SUB, DH), BF16),
            vmem((2, SH, SUB, DH), BF16),
            vmem((ROWS, ROWS), F32),
            vmem((2, ROWS, ROWS), F32),
            vmem((2, ROWS, ROWS), BF16),
            vmem((2, ROWS, ROWS), BF16),
            vmem((2, POS, POS), BF16),
            vmem((2, POS, POS), BF16),
            vmem((4, CTX, 2, SUB, DH), BF16),
            vmem((4, SH, NY, SUB, DH), BF16),
            *[vmem((HEADS, NY, SUB, DH), BF16)] * 4,
            vmem((4, SH, BLK, width), BF16),
            dma((len(CHUNKS),)), dma((len(CHUNKS),)),
            dma, dma((4,)), dma, dma((4,)), dma, dma, dma, dma((2,)),
            dma, dma, dma((4,)), dma, dma((4,)), dma, dma((2,)), dma, dma, pltpu.SemaphoreType.REGULAR((3,)),
        ],
        compiler_params=pltpu.CompilerParams(
            collective_id=0, has_side_effects=True, vmem_limit_bytes=24 << 20
        ),
        name="video_attention",
    )(*[pltpu.with_memory_space_constraint(x, pltpu.HBM) for x in (head_kind, frame_band, *local)])
    outs = pl.pallas_call(
        copy_kernel,
        out_shape=[jax.ShapeDtypeStruct((POS, width), BF16)] * 4,
        in_specs=[pl.BlockSpec(memory_space=pl.ANY)] * 4,
        out_specs=[pl.BlockSpec(memory_space=pltpu.HBM)] * 4,
        scratch_shapes=[dma((4,))],
        compiler_params=pltpu.CompilerParams(vmem_limit_bytes=4 << 20),
        name="copy_results",
    )(*outs)
    return tuple(x[None] for x in outs)


def solution(mesh):
    rows = P("ctx", None, "head")
    return jax.shard_map(
        body,
        mesh=mesh,
        in_specs=(rows, rows, rows, rows, P(), P()),
        out_specs=(rows, rows, rows, rows),
        check_vma=False,
    )
```

```python
import functools
import math

import jax
import jax.numpy as jnp
from jax import lax
from jax.experimental import pallas as pl
from jax.experimental.pallas import tpu as pltpu
from jax.sharding import PartitionSpec as P

DH = 128
HEADS = 24
NSPATIAL = 8
NTEMPORAL = 16
MESH = pl.DeviceIdType.MESH
NEG = -1e30
SCALE = DH ** -0.5
LOG2E = math.log2(math.e)

F32 = jnp.float32
BF16 = jnp.bfloat16

CTX = 32
NY = 4
SH = 8
LH = 3
POS = 512
BLK = 64
SUB = 16
ROWS = CTX * SUB

Q, K, V, G = 0, 1, 2, 3
ATT, QG, KG, VG = 0, 1, 2, 3
Z_ORDER = (4, 3, 5, 2, 6, 1, 7, 0)
CHUNKS = ((K, 0, 32), (K, 32, 32), (V, 0, 64), (Q, 0, 64), (G, 0, 64))


def dot_t(a, b):
    return lax.dot_general(a, b, (((1,), (1,)), ((), ())), preferred_element_type=F32)


def dot_n(a, b):
    return lax.dot_general(a, b, (((1,), (0,)), ((), ())), preferred_element_type=F32)


def t_dot(a, b):
    return lax.dot_general(a, b, (((0,), (0,)), ((), ())), preferred_element_type=F32)


def await_bytes(ref, sem):
    pltpu.make_async_copy(ref, ref, sem).wait()


def kernel(
    kind_ref, band_ref, q_hbm, k_hbm, v_hbm, g_hbm,
    att_hbm, qg_hbm, kg_hbm, vg_hbm,
    lists, got0, got1, got2, got3, got4, t_send, t_rows, s_send, s_rows, prior, prior_send, k_back, v_back, relay_up, relay_down,
    reach, t_weight, t_prob, t_dscore, s_prob, s_dscore, t_out, s_out, back0, back1, back2, back3, home_send,
    f1_send, f1_recv, t_sent, t_recv, s_sent, s_recv, p_sent, p_recv, b_sent, b_recv,
    rt_sent, rs_sent, r_recv, h_sent, h_recv, up_sent, up_recv, down_sent, down_recv, met,
):
    c = lax.axis_index("ctx")
    h = lax.axis_index("head")
    z = lax.div(c, NY)
    inputs = (q_hbm, k_hbm, v_hbm, g_hbm)
    outputs = (att_hbm, qg_hbm, kg_hbm, vg_hbm)
    gathered = (got0, got1, got2, got3, got4)
    results = (back0, back1, back2, back3)

    def ctx_peer(d):
        return lax.rem(c + d, CTX)

    def head_peer(d):
        return lax.rem(h + d, SH)

    def remote(src, dst, send, recv, ctx, head):
        pltpu.make_async_remote_copy(
            src_ref=src, dst_ref=dst, send_sem=send, recv_sem=recv,
            device_id=(ctx, head), device_id_type=MESH,
        ).start()

    barrier = pltpu.get_barrier_semaphore()

    @pl.loop(1, SH)
    def _(d):
        pl.semaphore_signal(barrier, inc=1, device_id=(c, head_peer(d)), device_id_type=MESH)

    y = lax.rem(c, NY)

    def y_peer(d):
        return z * NY + lax.rem(y + d, NY)

    def z_peer(d):
        return lax.rem(c + d * NY + CTX, CTX)

    for d in (1, -1):
        pl.semaphore_signal(barrier, inc=1, device_id=(z_peer(d), h), device_id_type=MESH)

    @pl.loop(1, NY)
    def _(d):
        pl.semaphore_signal(barrier, inc=1, device_id=(y_peer(d), h), device_id_type=MESH)

    pl.semaphore_wait(barrier, SH - 1 + 2 + NY - 1)

    def piece(n, shard, i):
        a, first, count = CHUNKS[n]
        return inputs[a].at[pl.ds(shard * BLK + first, count), pl.ds(i * DH, DH)]

    for n in range(len(CHUNKS)):
        @pl.loop(1, SH)
        def _(d):
            to = head_peer(d)
            for i in range(LH):
                remote(
                    piece(n, to, i), gathered[n].at[LH * h + i],
                    f1_send.at[n], f1_recv.at[n], c, to,
                )

    for n in range(len(CHUNKS)):
        for i in range(LH):
            pltpu.make_async_copy(
                piece(n, h, i), gathered[n].at[LH * h + i], f1_recv.at[n]
            ).start()

    kinds = [kind_ref[i] for i in range(HEADS)]
    so_far, count = [], jnp.int32(0)
    limits = [jnp.int32(0), jnp.int32(0)]
    for i in range(HEADS):
        spatial = kinds[i] == 1
        slot = jnp.where(spatial, NTEMPORAL + i - count, count)
        slot_in = jnp.minimum(slot, HEADS - 1)
        lists[32 + i] = slot_in
        lists[64 + i] = jnp.where(spatial, slot_in - NTEMPORAL, NSPATIAL)
        for e in range(2):
            limits[e] = jnp.where(slot == 2 * z + e, band_ref[i] * SUB, limits[e])
        count = count + jnp.where(spatial, 0, 1)
        so_far.append(count)
    for t in range(NTEMPORAL):
        before = sum((jnp.where(so_far[i] <= t, 1, 0) for i in range(HEADS)), jnp.int32(0))
        lists[t] = jnp.minimum(before, HEADS - 1)
    for s in range(NSPATIAL):
        before = sum((jnp.where(i + 1 - so_far[i] <= s, 1, 0) for i in range(HEADS)), jnp.int32(0))
        lists[NTEMPORAL + s] = jnp.minimum(before, HEADS - 1)

    @pl.loop(0, ROWS // 64)
    def _(b):
        row = lax.broadcasted_iota(jnp.int32, (64, ROWS), 0) + b * 64
        col = lax.broadcasted_iota(jnp.int32, (64, ROWS), 1)
        apart = row - col
        reach[pl.ds(b * 64, 64), :] = jnp.where(
            (apart & (SUB - 1)) == 0, jnp.abs(apart), ROWS * 2
        ).astype(F32)

    for far in (1, 2):
        for d in (far, -far):
            pl.semaphore_signal(
                met.at[far - 1], inc=1, device_id=(z_peer(d), h), device_id_type=MESH
            )
        pl.semaphore_wait(met.at[far - 1], 2)

    @pl.loop(1, NY)
    def _(d):
        pl.semaphore_signal(met.at[2], inc=1, device_id=(y_peer(d), h), device_id_type=MESH)

    pl.semaphore_wait(met.at[2], NY - 1)

    def await_chunk(n):
        await_bytes(gathered[n], f1_recv.at[n])

    def select_temporal(n):
        a, first, count = CHUNKS[n]
        subs = range(first // SUB, (first + count) // SUB)
        for pair in range(NTEMPORAL // 2):
            for e in range(2):
                block = gathered[n][lists[2 * pair + e]]
                for at, sub in enumerate(subs):
                    t_send[a, pair * NY + sub, e] = block[at * SUB:(at + 1) * SUB]

        for dz in Z_ORDER:
            @pl.loop(0, len(subs))
            def _(k):
                to = lax.rem(z + dz, CTX // NY) * NY + subs[0] + k
                if dz == 0:
                    @pl.when(to == c)
                    def _():
                        pltpu.make_async_copy(
                            t_send.at[a, c], t_rows.at[a, c], t_recv.at[a]
                        ).start()

                @pl.when(to != c)
                def _():
                    remote(t_send.at[a, to], t_rows.at[a, c], t_sent, t_recv.at[a], to, h)

    def select_spatial(n):
        a, first, count = CHUNKS[n]
        subs = range(first // SUB, (first + count) // SUB)
        for s in range(NSPATIAL):
            block = gathered[n][lists[NTEMPORAL + s]]
            s_send[a, s, pl.ds(subs[0], len(subs))] = block.reshape(len(subs), SUB, DH)
        if first + count < BLK:
            return
        pltpu.make_async_copy(s_send.at[a, h], s_rows.at[a, h], s_recv.at[a]).start()

        @pl.loop(1, SH)
        def _(d):
            to = head_peer(d)
            remote(s_send.at[a, to], s_rows.at[a, h], s_sent, s_recv.at[a], c, to)

    above = lax.rem(z + 1, CTX // NY) * NY
    below = lax.rem(z + CTX // NY - 1, CTX // NY) * NY + NY - 1

    def send_prior(a):
        i = a - K

        @pl.when(y < NY - 1)
        def _():
            @pl.loop(0, SH)
            def _(s):
                remote(s_send.at[a, s], prior.at[i, h], p_sent, p_recv, ctx_peer(1), s)

        @pl.when(y == NY - 1)
        def _():
            for r in range(NY - 1):
                remote(s_send.at[a, :, r], relay_up.at[i], p_sent, up_recv.at[i], z * NY + r, h)

            @pl.loop(0, SH)
            def _(s):
                remote(
                    s_send.at[a, s, NY - 1], prior.at[i, h, NY - 1], p_sent, p_recv, above, s
                )

    def pass_up(a):
        i = a - K

        @pl.when(y < NY - 1)
        def _():
            await_bytes(relay_up.at[i], up_recv.at[i])

            @pl.loop(0, SH)
            def _(s):
                remote(relay_up.at[i, s], prior.at[i, h, y], up_sent, p_recv, above, s)

    await_chunk(0)
    select_temporal(0)
    select_spatial(0)
    await_chunk(1)
    select_spatial(1)
    send_prior(K)
    select_temporal(1)
    await_chunk(2)
    select_spatial(2)
    send_prior(V)
    select_temporal(2)
    pass_up(K)
    await_chunk(3)
    select_temporal(3)
    select_spatial(3)
    pass_up(V)
    await_chunk(4)
    select_temporal(4)
    select_spatial(4)

    def t_block(a, e, first, frames):
        return t_rows[a, pl.ds(first, frames), e].reshape(frames * SUB, DH)

    def t_all(a, e):
        return t_block(a, e, 0, CTX)

    def send_temporal(o):
        mine = results[o].at[pl.ds(2 * z, 2), lax.rem(c, NY)]
        pltpu.make_async_copy(t_out.at[o, c], mine, r_recv.at[o]).start()

        for dz in Z_ORDER:
            @pl.loop(0 if dz else 1, NY)
            def _(k):
                to = lax.rem(z + dz, CTX // NY) * NY + lax.rem(y + k, NY)
                remote(t_out.at[o, to], mine, rt_sent, r_recv.at[o], to, h)

    def put(o, e, value):
        t_out[o, :, e] = value.astype(BF16).reshape(CTX, SUB, DH)

    await_bytes(t_rows.at[K], t_recv.at[K])
    await_bytes(t_rows.at[Q], t_recv.at[Q])
    for e in range(2):
        keys = t_all(K, e)
        for part in range(2):
            score = dot_t(t_block(Q, e, part * 16, 16), keys) * (SCALE * LOG2E)
            rows = pl.ds(part * 256, 256)
            score = score + jnp.minimum(limits[e].astype(F32) - reach[rows, :], 0.0) * -NEG
            top = jnp.max(score, axis=-1, keepdims=True)
            weight = jnp.exp2(score - top)
            weight = weight * (1.0 / jnp.sum(weight, axis=-1, keepdims=True))
            t_weight[e, rows, :] = weight
            t_prob[e, rows, :] = weight.astype(BF16)
    await_bytes(t_rows.at[V], t_recv.at[V])
    for e in range(2):
        put(ATT, e, dot_n(t_prob[e], t_all(V, e)))
    send_temporal(ATT)

    for a in range(4):
        await_bytes(s_rows.at[a], s_recv.at[a])
    await_bytes(prior, p_recv)
    k_own = s_rows[K].reshape(POS, DH)
    v_own = s_rows[V].reshape(POS, DH)
    k_prior = prior[0].reshape(POS, DH)
    v_prior = prior[1].reshape(POS, DH)
    part_rows = 256
    part_blocks = part_rows // BLK

    @pl.loop(0, POS // part_rows)
    def _(part):
        rows = pl.ds(part * part_rows, part_rows)
        blocks = pl.ds(part * part_blocks, part_blocks)
        q = s_rows[Q, blocks].reshape(part_rows, DH)
        g = s_rows[G, blocks].reshape(part_rows, DH)
        old = dot_t(q, k_prior) * (SCALE * LOG2E)
        old = jnp.where(c > 0, old, NEG)
        own = dot_t(q, k_own) * (SCALE * LOG2E)
        top = jnp.maximum(
            jnp.max(old, axis=-1, keepdims=True), jnp.max(own, axis=-1, keepdims=True)
        )
        old = jnp.exp2(old - top)
        own = jnp.exp2(own - top)
        inverse = 1.0 / (
            jnp.sum(old, axis=-1, keepdims=True) + jnp.sum(own, axis=-1, keepdims=True)
        )
        old = old * inverse
        own = own * inverse
        old_prob = old.astype(BF16)
        own_prob = own.astype(BF16)
        s_prob[0, rows, :] = old_prob
        s_prob[1, rows, :] = own_prob
        attended = (dot_n(old_prob, v_prior) + dot_n(own_prob, v_own)).astype(BF16)
        s_out[ATT, blocks] = attended.reshape(part_blocks, NY, SUB, DH)
        delta = jnp.sum(g.astype(F32) * attended.astype(F32), axis=-1, keepdims=True)
        old_ds = (old * (dot_t(g, v_prior) - delta) * SCALE).astype(BF16)
        own_ds = (own * (dot_t(g, v_own) - delta) * SCALE).astype(BF16)
        s_dscore[0, rows, :] = old_ds
        s_dscore[1, rows, :] = own_ds
        qg = (dot_n(old_ds, k_prior) + dot_n(own_ds, k_own)).astype(BF16)
        s_out[QG, blocks] = qg.reshape(part_blocks, NY, SUB, DH)

    def send_spatial(o):
        pltpu.make_async_copy(s_out.at[o, h], results[o].at[NTEMPORAL + h], r_recv.at[o]).start()

        @pl.loop(1, SH)
        def _(d):
            to = head_peer(d)
            remote(
                s_out.at[o, to], results[o].at[NTEMPORAL + h], rs_sent, r_recv.at[o], c, to
            )

    q_all = s_rows[Q].reshape(POS, DH)
    g_all = s_rows[G].reshape(POS, DH)
    prior_send[0] = t_dot(s_dscore[0], q_all).astype(BF16).reshape(SH, NY, SUB, DH)
    prior_send[1] = t_dot(s_prob[0], g_all).astype(BF16).reshape(SH, NY, SUB, DH)
    for i, back in enumerate((k_back, v_back)):
        @pl.when(y > 0)
        def _():
            @pl.loop(0, SH)
            def _(s):
                remote(prior_send.at[i, s], back.at[h], b_sent, b_recv.at[i], ctx_peer(CTX - 1), s)

        @pl.when(y == 0)
        def _():
            for r in range(1, NY):
                remote(
                    prior_send.at[i, :, r], relay_down.at[i], b_sent, down_recv, z * NY + r, h
                )

            @pl.loop(0, SH)
            def _(s):
                remote(prior_send.at[i, s, 0], back.at[h, 0], b_sent, b_recv.at[i], below, s)

    s_out[KG] = t_dot(s_dscore[1], q_all).astype(BF16).reshape(SH, NY, SUB, DH)
    s_out[VG] = t_dot(s_prob[1], g_all).astype(BF16).reshape(SH, NY, SUB, DH)
    for o in (ATT, QG, VG, KG):
        send_spatial(o)

    await_bytes(t_rows.at[G], t_recv.at[G])
    for e in range(2):
        values = t_all(V, e)
        keys = t_all(K, e)
        for part in range(2):
            rows = pl.ds(part * 256, 256)
            g = t_block(G, e, part * 16, 16)
            attended = t_out[ATT, pl.ds(part * 16, 16), e].reshape(256, DH)
            delta = jnp.sum(g.astype(F32) * attended.astype(F32), axis=-1, keepdims=True)
            dscore = t_weight[e, rows, :] * (dot_t(g, values) - delta) * SCALE
            t_dscore[e, rows, :] = dscore.astype(BF16)
        put(QG, e, dot_n(t_dscore[e], keys))
    send_temporal(QG)
    @pl.when(y > 0)
    def _():
        await_bytes(relay_down, down_recv)
        for i, back in enumerate((k_back, v_back)):
            @pl.loop(0, SH)
            def _(s):
                remote(relay_down.at[i, s], back.at[h, y], down_sent, b_recv.at[i], below, s)

    for e in range(2):
        put(VG, e, t_dot(t_prob[e], t_all(G, e)))
    send_temporal(VG)

    def send_home(o):
        await_bytes(results[o], r_recv.at[o])
        for head in range(HEADS):
            block = results[o][lists[32 + head]].reshape(BLK, DH)
            if o in (KG, VG):
                back = (k_back if o == KG else v_back)[lists[64 + head]].reshape(BLK, DH)
                block = (block.astype(F32) + back.astype(F32)).astype(BF16)
            shard, column = divmod(head, LH)
            home_send[o, shard, :, column * DH:(column + 1) * DH] = block
        mine = pl.ds(h * BLK, BLK)
        pltpu.make_async_copy(home_send.at[o, h], outputs[o].at[mine, :], h_recv.at[o]).start()

        @pl.loop(1, SH)
        def _(d):
            to = head_peer(d)
            remote(home_send.at[o, to], outputs[o].at[mine, :], h_sent, h_recv.at[o], c, to)

    for e in range(2):
        put(KG, e, t_dot(t_dscore[e], t_all(Q, e)))
    send_home(ATT)
    send_temporal(KG)

    send_home(QG)
    for back in (k_back, v_back):
        back[NSPATIAL] = jnp.zeros((NY, SUB, DH), BF16)
    for i, back in enumerate((k_back, v_back)):
        await_bytes(back.at[pl.ds(0, NSPATIAL)], b_recv.at[i])
    send_home(VG)
    send_home(KG)

    for o in range(4):
        await_bytes(outputs[o], h_recv.at[o])
    for n in range(len(CHUNKS)):
        await_bytes(gathered[n].at[pl.ds(0, HEADS - LH)], f1_send.at[n])
    await_bytes(t_rows.at[:, pl.ds(0, CTX - 1)], t_sent)
    await_bytes(s_rows.at[:, pl.ds(0, SH - 1)], s_sent)
    await_bytes(prior, p_sent)
    await_bytes(prior_send, b_sent)

    @pl.when(y < NY - 1)
    def _():
        await_bytes(relay_up, up_sent)

    @pl.when(y > 0)
    def _():
        await_bytes(relay_down, down_sent)

    await_bytes(t_out.at[:, pl.ds(0, CTX - 1)], rt_sent)
    await_bytes(s_out.at[:, pl.ds(0, SH - 1)], rs_sent)
    await_bytes(home_send.at[:, pl.ds(0, SH - 1)], h_sent)


def copy_kernel(*refs):
    sources, targets, sem = refs[:4], refs[4:8], refs[8]
    copies = [pltpu.make_async_copy(x, y, sem.at[o]) for o, (x, y) in enumerate(zip(sources, targets))]
    for copy in copies:
        copy.start()
    for copy in copies:
        copy.wait()


def body(queries, key_rows, value_rows, out_grad, head_kind, frame_band):
    width = LH * DH
    local = [x.reshape(POS, width) for x in (queries, key_rows, value_rows, out_grad)]
    vmem = pltpu.VMEM
    dma = pltpu.SemaphoreType.DMA
    outs = pl.pallas_call(
        kernel,
        out_shape=[jax.ShapeDtypeStruct((POS, width), BF16)] * 4,
        in_specs=[pl.BlockSpec(memory_space=pltpu.SMEM)] * 2
        + [pl.BlockSpec(memory_space=pl.ANY)] * 4,
        out_specs=[pl.BlockSpec(memory_space=pl.ANY)] * 4,
        scratch_shapes=[
            pltpu.SMEM((96,), jnp.int32),
            *[vmem((HEADS, count, DH), BF16) for _, _, count in CHUNKS],
            vmem((4, CTX, 2, SUB, DH), BF16),
            vmem((4, CTX, 2, SUB, DH), BF16),
            vmem((4, SH, NY, SUB, DH), BF16),
            vmem((4, SH, NY, SUB, DH), BF16),
            vmem((2, SH, NY, SUB, DH), BF16),
            vmem((2, SH, NY, SUB, DH), BF16),
            *[vmem((NSPATIAL + 1, NY, SUB, DH), BF16)] * 2,
            vmem((2, SH, SUB, DH), BF16),
            vmem((2, SH, SUB, DH), BF16),
            vmem((ROWS, ROWS), F32),
            vmem((2, ROWS, ROWS), F32),
            vmem((2, ROWS, ROWS), BF16),
            vmem((2, ROWS, ROWS), BF16),
            vmem((2, POS, POS), BF16),
            vmem((2, POS, POS), BF16),
            vmem((4, CTX, 2, SUB, DH), BF16),
            vmem((4, SH, NY, SUB, DH), BF16),
            *[vmem((HEADS, NY, SUB, DH), BF16)] * 4,
            vmem((4, SH, BLK, width), BF16),
            dma((len(CHUNKS),)), dma((len(CHUNKS),)),
            dma, dma((4,)), dma, dma((4,)), dma, dma, dma, dma((2,)),
            dma, dma, dma((4,)), dma, dma((4,)), dma, dma((2,)), dma, dma, pltpu.SemaphoreType.REGULAR((3,)),
        ],
        compiler_params=pltpu.CompilerParams(
            collective_id=0, has_side_effects=True, vmem_limit_bytes=24 << 20
        ),
        name="video_attention",
    )(*[pltpu.with_memory_space_constraint(x, pltpu.HBM) for x in (head_kind, frame_band, *local)])
    outs = pl.pallas_call(
        copy_kernel,
        out_shape=[jax.ShapeDtypeStruct((POS, width), BF16)] * 4,
        in_specs=[pl.BlockSpec(memory_space=pl.ANY)] * 4,
        out_specs=[pl.BlockSpec(memory_space=pltpu.HBM)] * 4,
        scratch_shapes=[dma((4,))],
        compiler_params=pltpu.CompilerParams(vmem_limit_bytes=4 << 20),
        name="copy_results",
    )(*outs)
    return tuple(x[None] for x in outs)


def solution(mesh):
    rows = P("ctx", None, "head")
    return jax.shard_map(
        body,
        mesh=mesh,
        in_specs=(rows, rows, rows, rows, P(), P()),
        out_specs=(rows, rows, rows, rows),
        check_vma=False,
    )
```
